32 devices in a mesh: tile: 8 (over y, x, core), grp: 4 (over z).
Axes of the slice: x: 2, y: 2, z: 4, core: 2. Of those that a mesh axis runs over, the one named last changes fastest.
Arguments:
- earlier_flow_speeds: float32 [2, 64, 256, 512], P(None, None, 'tile', 'grp'), may hold values from -6 to 6
- flow_rate_factor: float32 [64, 256, 512], P(None, 'tile', 'grp'), may hold values from 0.5 to 2
- scaled_warmth: float32 [64, 256, 512], P('grp', 'tile'), may hold values from -3 to 3
- gravity_forcing: float32 [2, 256, 512], P(None, 'tile', 'grp'), may hold values from -6 to 6
- sliding_coefficient: float32 [256, 512], P('tile', 'grp'), may hold values from 1 to 10
- icy_column_flag: int32 [256, 512], P('tile', 'grp'), may hold values 0 or 1
- resting_on_bed_flag: int32 [256, 512], P('tile', 'grp'), may hold values 0 or 1
Outputs:
- velocity: float32 [2, 64, 256, 512], P(None, None, 'tile', 'grp')
- temperature_next: float32 [64, 256, 512], P('grp', 'tile')
- hardness_next: float32 [64, 256, 512], P(None, 'tile', 'grp')
The draws below stay inside these ranges and needn't reach their ends.
All inputs are finite; a program needn't handle non-finite values. No bound on the sum of `icy_column_flag` or of `resting_on_bed_flag` on one device may be relied on, other than what follows from the above.
Results may differ from the reference program's by a relative error of at most 0.00002.
Values sent between devices are 32-bit elements; how exact they have to be, the bound alone decides.
A program may use at most 64 MiB of HBM per device.

```python
import math
import jax
import jax.numpy as jnp
from jax import lax

STRATA_NUMBER = 64
SWEEPS = 4
SECTIONS = 4
ZONAL_SPAN = 256
MERIDIONAL_SPAN = 512


def place_ends(array, own_key, low, largest):
    shape = array.shape
    place = [jax.random.randint(jax.random.fold_in(own_key, axis), (), 0, shape[axis]) for axis in range(len(shape))]
    array = array.at[tuple(place)].set(low)
    longest = shape.index(max(shape))
    place[longest] = (place[longest] + 1) % shape[longest]
    return array.at[tuple(place)].set(largest)


def block_scale(stream_key, extent, shards, smallest, largest):
    def one(dim, parts):
        steps = jax.random.uniform(jax.random.fold_in(jax.random.fold_in(stream_key, 6), dim), (parts,), jnp.float32, smallest / len(shards), largest / len(shards))
        return jnp.repeat(jnp.exp(steps), extent[dim] // parts).reshape((-1,) + (1,) * (len(extent) - dim - 1))

    factor_of = one(*shards[0])
    for cut in shards[1:]:
        factor_of = factor_of * one(*cut)
    return factor_of


def gaussian(stream_key, shape, scale, most, split=(), dtype=jnp.bfloat16):
    gain = block_scale(stream_key, shape, split, -0.22, 0.18) if split else 1.0
    entries = jax.random.normal(stream_key, shape, jnp.float32) * scale * gain
    return jnp.minimum(jnp.maximum(entries, -most), most).astype(dtype)


def setup_inputs(seed: int = 0) -> dict:
    arg_keys = jax.random.split(jax.random.key(seed), 8)
    earlier_flow_speeds = gaussian(arg_keys[0], (2, STRATA_NUMBER, ZONAL_SPAN, MERIDIONAL_SPAN), 1.0, 6.0, ((2, 8), (3, 4)), jnp.float32)
    flow_rate_factor = jnp.clip(jnp.exp(math.log(2.0) - 1.3862944 * jax.random.uniform(arg_keys[1], (STRATA_NUMBER, ZONAL_SPAN, MERIDIONAL_SPAN), jnp.float32) ** block_scale(arg_keys[1], (STRATA_NUMBER, ZONAL_SPAN, MERIDIONAL_SPAN), ((1, 8), (2, 4)), -0.2, 0.2)), 0.5, 2.0)
    scaled_warmth = gaussian(arg_keys[2], (STRATA_NUMBER, ZONAL_SPAN, MERIDIONAL_SPAN), 0.5, 3.0, ((0, 4), (1, 8)), jnp.float32)
    gravity_forcing = gaussian(arg_keys[3], (2, ZONAL_SPAN, MERIDIONAL_SPAN), 1.0, 6.0, ((1, 8), (2, 4)), jnp.float32)
    sliding_coefficient = jnp.clip(jnp.exp(math.log(10.0) - 2.3025851 * jax.random.uniform(arg_keys[4], (ZONAL_SPAN, MERIDIONAL_SPAN), jnp.float32) ** block_scale(arg_keys[4], (ZONAL_SPAN, MERIDIONAL_SPAN), ((0, 8), (1, 4)), -0.2, 0.2)), 1.0, 10.0)
    icy_column_flag = place_ends((jax.random.randint(arg_keys[5], (ZONAL_SPAN, MERIDIONAL_SPAN), 0, 4) < 3).astype(jnp.int32), jax.random.fold_in(arg_keys[5], 1), 0, 1)
    resting_on_bed_flag = place_ends((jax.random.randint(arg_keys[6], (ZONAL_SPAN, MERIDIONAL_SPAN), 0, 2) < 1).astype(jnp.int32), jax.random.fold_in(arg_keys[6], 1), 0, 1)
    return {"earlier_flow_speeds": earlier_flow_speeds, "flow_rate_factor": flow_rate_factor, "scaled_warmth": scaled_warmth, "gravity_forcing": gravity_forcing, "sliding_coefficient": sliding_coefficient, "icy_column_flag": icy_column_flag, "resting_on_bed_flag": resting_on_bed_flag}


vertical_weight = 4.0
strain_floor = 0.01
cross_weight = 0.75
diag_weight = 22.0
diffuse_flat = 0.1
diffuse_vert = 0.2
advect_weight = 0.05
heat_weight = 0.05
arrhenius = 0.6


def level_pad(field):
    return jnp.concatenate([field[:1], field, field[-1:]], axis=0)


def strain_parts(padded_u, padded_v):
    center_u = padded_u[:, 1:-1, 1:-1]
    center_v = padded_v[:, 1:-1, 1:-1]
    strain_xx = 0.5 * (padded_u[:, 2:, 1:-1] - padded_u[:, :-2, 1:-1])
    shear_uy = 0.5 * (padded_u[:, 1:-1, 2:] - padded_u[:, 1:-1, :-2])
    shear_vx = 0.5 * (padded_v[:, 2:, 1:-1] - padded_v[:, :-2, 1:-1])
    strain_yy = 0.5 * (padded_v[:, 1:-1, 2:] - padded_v[:, 1:-1, :-2])
    column_u = level_pad(center_u)
    column_v = level_pad(center_v)
    vert_u = 0.5 * (column_u[2:] - column_u[:-2])
    vert_v = 0.5 * (column_v[2:] - column_v[:-2])
    shear = shear_uy + shear_vx
    effective = (strain_xx * strain_xx + strain_yy * strain_yy + strain_xx * strain_yy
                 + 0.25 * shear * shear + 0.25 * (vert_u * vert_u + vert_v * vert_v))
    return effective, column_u, column_v


def viscosity_of(flow_rate_factor, effective):
    return flow_rate_factor * jnp.power(effective + strain_floor, -1.0 / 3.0)


def jacobi_sweep(padded_u, padded_v, flow_rate_factor, drive_u, driving_stress_north, drag_base, ice):
    effective, column_u, column_v = strain_parts(padded_u, padded_v)
    viscosity = viscosity_of(flow_rate_factor, effective)
    levels = padded_u.shape[0]
    bottom = (lax.broadcasted_iota(jnp.int32, (levels, 1, 1), 0) == 0).astype(jnp.float32)
    diagonal = viscosity * diag_weight + bottom * drag_base[None]
    near_u = (4.0 * (padded_u[:, 2:, 1:-1] + padded_u[:, :-2, 1:-1])
              + (padded_u[:, 1:-1, 2:] + padded_u[:, 1:-1, :-2])
              + vertical_weight * (column_u[2:] + column_u[:-2]))
    near_v = ((padded_v[:, 2:, 1:-1] + padded_v[:, :-2, 1:-1])
              + 4.0 * (padded_v[:, 1:-1, 2:] + padded_v[:, 1:-1, :-2])
              + vertical_weight * (column_v[2:] + column_v[:-2]))
    cross_u = cross_weight * (padded_v[:, 2:, 2:] - padded_v[:, :-2, 2:] - padded_v[:, 2:, :-2] + padded_v[:, :-2, :-2])
    cross_v = cross_weight * (padded_u[:, 2:, 2:] - padded_u[:, :-2, 2:] - padded_u[:, 2:, :-2] + padded_u[:, :-2, :-2])
    guard = diagonal + (1.0 - ice[None])
    new_u = ice[None] * (drive_u[None] + viscosity * (near_u + cross_u)) / guard
    new_v = ice[None] * (driving_stress_north[None] + viscosity * (near_v + cross_v)) / guard
    return jnp.stack([new_u, new_v])


def heating(padded_u, padded_v, flow_rate_factor, ice):
    effective, column_u, column_v = strain_parts(padded_u, padded_v)
    return ice[None] * 2.0 * viscosity_of(flow_rate_factor, effective) * effective


def thermal_section(padded, speed_u, speed_v, heat):
    center = padded[1:-1, 1:-1, 1:-1]
    east = padded[1:-1, 2:, 1:-1]
    west = padded[1:-1, :-2, 1:-1]
    north = padded[1:-1, 1:-1, 2:]
    south = padded[1:-1, 1:-1, :-2]
    upper = padded[2:, 1:-1, 1:-1]
    lower = padded[:-2, 1:-1, 1:-1]
    advect = (jnp.maximum(speed_u, 0.0) * (center - west) + jnp.minimum(speed_u, 0.0) * (east - center)
              + jnp.maximum(speed_v, 0.0) * (center - south) + jnp.minimum(speed_v, 0.0) * (north - center))
    return (center + diffuse_flat * (east + west + north + south - 4.0 * center)
            + diffuse_vert * (upper + lower - 2.0 * center) - advect_weight * advect + heat_weight * heat)


def reference(earlier_flow_speeds, flow_rate_factor, scaled_warmth, gravity_forcing, sliding_coefficient, icy_column_flag, resting_on_bed_flag):
    ice = icy_column_flag.astype(jnp.float32)
    drag_base = sliding_coefficient * resting_on_bed_flag.astype(jnp.float32)
    current = earlier_flow_speeds
    for sweep in range(SWEEPS):
        padded = jnp.pad(current, ((0, 0), (0, 0), (1, 1), (1, 1)))
        current = jacobi_sweep(padded[0], padded[1], flow_rate_factor, gravity_forcing[0], gravity_forcing[1], drag_base, ice)
    padded = jnp.pad(current, ((0, 0), (0, 0), (1, 1), (1, 1)))
    heat = heating(padded[0], padded[1], flow_rate_factor, ice)
    heat_content_field = scaled_warmth
    for section in range(SECTIONS):
        heat_content_field = thermal_section(jnp.pad(heat_content_field, 1), current[0], current[1], heat)
    return current, heat_content_field, jnp.exp(-arrhenius * heat_content_field)
```

```python
import functools

import jax
import jax.numpy as jnp
from jax import lax
from jax.experimental import pallas as pl
from jax.experimental.pallas import tpu as pltpu
from jax.sharding import PartitionSpec as P

SWEEPS = 4
SECTIONS = 4
LANES = 128
SUB = 8
PAD = 8

MESH = pl.DeviceIdType.MESH


def roll(x, shift, axis=1):
    return pltpu.roll(x, shift, axis)


def kernel(
    n,
    m,
    R,
    L,
    LG,
    vel_in,
    rate_in,
    warm_in,
    grav,
    slide,
    icy,
    bed,
    vel_out,
    temp_out,
    hard_out,
    vel_st,
    rate_st,
    warm_st,
    hard_st,
    U,
    DY,
    SY,
    T,
    Q,
    pk,
    dk,
    row_rx,
    col_rx,
    diag_rx,
    tpk,
    trow_rx,
    tcol_rx,
    loc_sem,
    vs_sem,
    vr_sem,
    ts_sem,
    tr_sem,
    ws_sem,
    wr_sem,
    os_sem,
    or_sem,
):
    t = lax.axis_index("tile")
    g = lax.axis_index("grp")
    LB = L // SUB
    f32 = jnp.float32

    vel_cp = [
        pltpu.make_async_copy(vel_in.at[f], vel_st.at[f], loc_sem.at[f]) for f in range(2)
    ]
    rate_cp = pltpu.make_async_copy(rate_in, rate_st, loc_sem.at[2])
    for cp in vel_cp:
        cp.start()
    rate_cp.start()

    lo_t, hi_t, lo_g, hi_g = t > 0, t < n - 1, g > 0, g < m - 1

    def has(dt, dg):
        ok = None
        for d, lo, hi in ((dt, lo_t, hi_t), (dg, lo_g, hi_g)):
            if d:
                c = lo if d < 0 else hi
                ok = c if ok is None else jnp.logical_and(ok, c)
        return ok

    for ref in (row_rx, col_rx, diag_rx, trow_rx, tcol_rx):
        ref[...] = jnp.zeros_like(ref)

    barrier = pltpu.get_barrier_semaphore()
    around = [(-1, -1), (-1, 0), (-1, 1), (1, -1), (1, 0), (1, 1)]
    for dt, dg in around:

        @pl.when(has(dt, dg))
        def _(dt=dt, dg=dg):
            pl.semaphore_signal(
                barrier, inc=1, device_id=(t + dt, g + dg), device_id_type=MESH
            )

    for d in range(1, m):
        pl.semaphore_signal(
            barrier, inc=1, device_id=(t, lax.rem(g + d, m)), device_id_type=MESH
        )

    sides_t = lo_t.astype(jnp.int32) + hi_t.astype(jnp.int32)
    sides_g = lo_g.astype(jnp.int32) + hi_g.astype(jnp.int32)
    pl.semaphore_wait(barrier, m - 1 + sides_t * (1 + sides_g))

    def warm_copy(d):
        to = lax.rem(g + d, m)
        src = warm_in.at[:, :, pl.ds(pl.multiple_of(to * LANES, LANES), LANES)]
        dst = warm_st.at[pl.ds(g * LG, LG)]
        if d == 0:
            return pltpu.make_async_copy(src, dst, loc_sem.at[3])
        return pltpu.make_async_remote_copy(
            src, dst, ws_sem.at[d], wr_sem.at[d], device_id=(t, to), device_id_type=MESH
        )

    lane = lax.broadcasted_iota(jnp.int32, (SUB, LANES), 1)
    subl = lax.broadcasted_iota(jnp.int32, (SUB, LANES), 0)
    first = lane == 0
    last = lane == LANES - 1
    odd = lax.rem(lane, 2) == 1
    half = LANES // 2
    u_edge = jnp.logical_or(first, last)

    def back(x, extra=0):
        return lax.rem(2 * LANES - 2 * x - extra, LANES)

    def near_lane(x, shift):
        lane_x = lax.rem(lane + (LANES + 1) - shift, LANES)
        return lane_x < 2

    def vel_moves(k):
        slot = k % 2
        moves = [
            ((1, 0), U.at[slot, :, R, PAD : PAD + L, :], row_rx.at[k, 0]),
            ((-1, 0), U.at[slot, :, 1, PAD : PAD + L, :], row_rx.at[k, 1]),
            ((0, 1), pk.at[k], col_rx.at[k, 0]),
            ((0, -1), pk.at[k], col_rx.at[k, 1]),
        ]
        if k < SWEEPS:
            moves += [
                ((1, 1), dk.at[k, 1], diag_rx.at[k, 0, 0]),
                ((1, -1), dk.at[k, 1], diag_rx.at[k, 0, 1]),
                ((-1, 1), dk.at[k, 0], diag_rx.at[k, 1, 0]),
                ((-1, -1), dk.at[k, 0], diag_rx.at[k, 1, 1]),
            ]
        return moves

    def start(moves, s_sem, r_sem):
        for j, ((dt, dg), src, dst) in enumerate(moves):

            @pl.when(has(dt, dg))
            def _(j=j, dt=dt, dg=dg, src=src, dst=dst):
                pltpu.make_async_remote_copy(
                    src,
                    dst,
                    s_sem.at[j],
                    r_sem.at[j],
                    device_id=(t + dt, g + dg),
                    device_id_type=MESH,
                ).start()

    def finish(moves, s_sem, r_sem):
        for j, ((dt, dg), src, dst) in enumerate(moves):

            @pl.when(has(dt, dg))
            def _(j=j, dt=dt, dg=dg, src=src, dst=dst):
                pltpu.make_async_remote_copy(
                    src,
                    dst,
                    s_sem.at[j],
                    r_sem.at[j],
                    device_id=(t + dt, g + dg),
                    device_id_type=MESH,
                ).wait_send()

            @pl.when(has(-dt, -dg))
            def _(j=j, dt=dt, dg=dg, src=src, dst=dst):
                pltpu.make_async_remote_copy(
                    src,
                    dst,
                    s_sem.at[j],
                    r_sem.at[j],
                    device_id=(t - dt, g - dg),
                    device_id_type=MESH,
                ).wait_recv()

    def put_vel(slot, k, x, b, values):
        lv = PAD + b * SUB
        for f in range(2):
            U[slot, f, x + 1, lv : lv + SUB, :] = values[f]
            if b == 0:
                U[slot, f, x + 1, lv - 1 : lv, :] = values[f][0:1]
            if b == LB - 1:
                U[slot, f, x + 1, lv + SUB : lv + SUB + 1, :] = values[f][SUB - 1 : SUB]
        w = jnp.where(u_edge, values[0], roll(values[1], half))
        w = roll(w, 2 * x)
        hit = jnp.logical_or(near_lane(x, 2 * x), near_lane(x, 2 * x + half))
        bl = b * SUB
        pk[k, bl : bl + SUB, :] = jnp.where(hit, w, pk[k, bl : bl + SUB, :])

    def put_diag(slot, k):
        for side, x in ((0, 1), (1, R)):
            acc = jnp.zeros((SUB, LANES), f32)
            for b in range(LB):
                lv = PAD + b * SUB
                u = U[slot, 0, x, lv : lv + SUB, :]
                v = U[slot, 1, x, lv : lv + SUB, :]
                w = jnp.where(u_edge, u, roll(v, half))
                w = roll(w, 2 * b) if b else w
                hit = jnp.logical_or(near_lane(b, 2 * b), near_lane(b, 2 * b + half))
                acc = jnp.where(hit, w, acc)
            dk[k, side] = acc

    def fill_level_pads(slot, row):
        for f in range(2):
            U[slot, f, row, PAD - 1 : PAD, :] = U[slot, f, row, PAD : PAD + 1, :]
            U[slot, f, row, PAD + L : PAD + L + 1, :] = U[
                slot, f, row, PAD + L - 1 : PAD + L, :
            ]

    def lane_parts(f, row, b, u, edge):
        up = roll(jnp.where(first, edge, u), LANES - 1)
        down = roll(jnp.where(last, edge, u), 1)
        bl = b * SUB
        DY[f, row, bl : bl + SUB, :] = up - down
        return up + down, bl

    def prepare(k):
        slot = k % 2
        for side, row in ((0, 0), (1, R + 1)):
            for f in range(2):
                U[slot, f, row, PAD : PAD + L, :] = row_rx[k, side, f]
            if k < SWEEPS:
                corner = jnp.where(odd, diag_rx[k, side, 0], diag_rx[k, side, 1])
                for b in range(LB):
                    lv = PAD + b * SUB
                    for f in range(2):
                        edge = roll(corner, (2 * LANES - 2 * b - f * half) % LANES)
                        lane_parts(f, row, b, U[slot, f, row, lv : lv + SUB, :], edge)

        def body(x, c):
            for b in range(LB):
                lv = PAD + b * SUB
                bl = b * SUB
                halo = jnp.where(
                    odd, col_rx[k, 0, bl : bl + SUB, :], col_rx[k, 1, bl : bl + SUB, :]
                )
                for f in range(2):
                    edge = roll(halo, back(x, f * half))
                    u = U[slot, f, x + 1, lv : lv + SUB, :]
                    s, _ = lane_parts(f, x + 1, b, u, edge)
                    if k < SWEEPS:
                        SY[f, x, bl : bl + SUB, :] = s
            return c

        lax.fori_loop(0, R, body, 0)

    def strain(slot, x, b):
        lv = PAD + b * SUB
        bl = b * SUB
        ue = U[slot, 0, x + 2, lv : lv + SUB, :]
        uw = U[slot, 0, x, lv : lv + SUB, :]
        ve = U[slot, 1, x + 2, lv : lv + SUB, :]
        vw = U[slot, 1, x, lv : lv + SUB, :]
        uu = U[slot, 0, x + 1, lv + 1 : lv + 1 + SUB, :]
        ul = U[slot, 0, x + 1, lv - 1 : lv - 1 + SUB, :]
        vu = U[slot, 1, x + 1, lv + 1 : lv + 1 + SUB, :]
        vl = U[slot, 1, x + 1, lv - 1 : lv - 1 + SUB, :]
        dyu = DY[0, x + 1, bl : bl + SUB, :]
        dyv = DY[1, x + 1, bl : bl + SUB, :]
        xx = ue - uw
        shear = dyu + (ve - vw)
        du = uu - ul
        dv = vu - vl
        effective = 0.25 * (
            xx * xx + dyv * dyv + xx * dyv + 0.25 * (shear * shear + du * du + dv * dv)
        )
        rate = Q[1, x, bl : bl + SUB, :]
        viscosity = rate * jnp.exp(jnp.log(effective + 0.01) * (-1.0 / 3.0))
        return effective, viscosity, ue + uw, ve + vw, uu + ul, vu + vl

    def sweep(k):
        slot = k % 2
        new_slot = (k + 1) % 2

        def body(x, c):
            ice = icy[pl.ds(x, 1), :].astype(f32)
            drag = slide[pl.ds(x, 1), :] * bed[pl.ds(x, 1), :].astype(f32)
            water = 1.0 - ice
            gu = grav[0, pl.ds(x, 1), :]
            gv = grav[1, pl.ds(x, 1), :]
            for b in range(LB):
                bl = b * SUB
                _, visc, sxu, sxv, szu, szv = strain(slot, x, b)
                diagonal = 22.0 * visc + water
                if b == 0:
                    diagonal = diagonal + jnp.where(subl == 0, drag, 0.0)
                cross_u = DY[1, x + 2, bl : bl + SUB, :] - DY[1, x, bl : bl + SUB, :]
                cross_v = DY[0, x + 2, bl : bl + SUB, :] - DY[0, x, bl : bl + SUB, :]
                near_u = 4.0 * (sxu + szu) + SY[0, x, bl : bl + SUB, :] + 0.75 * cross_u
                near_v = (
                    sxv + 4.0 * (SY[1, x, bl : bl + SUB, :] + szv) + 0.75 * cross_v
                )
                scale = ice / diagonal
                new_u = (gu + visc * near_u) * scale
                new_v = (gv + visc * near_v) * scale
                put_vel(new_slot, k + 1, x, b, (new_u, new_v))
                if k == SWEEPS - 1:
                    place = pl.ds(bl * R + x, SUB, stride=R)
                    vel_flat[0][place, :] = new_u
                    vel_flat[1][place, :] = new_v
            return c

        lax.fori_loop(0, R, body, 0)

    def th_moves(k):
        slot = k % 2
        return [
            ((1, 0), T.at[slot, R, PAD : PAD + L, :], trow_rx.at[k, 0]),
            ((-1, 0), T.at[slot, 1, PAD : PAD + L, :], trow_rx.at[k, 1]),
            ((0, 1), tpk.at[k], tcol_rx.at[k, 0]),
            ((0, -1), tpk.at[k], tcol_rx.at[k, 1]),
        ]

    def put_theta(slot, k, x, b, value):
        lv = PAD + b * SUB
        bl = b * SUB
        T[slot, x + 1, lv : lv + SUB, :] = value
        w = roll(value, 2 * x)
        tpk[k, bl : bl + SUB, :] = jnp.where(
            near_lane(x, 2 * x), w, tpk[k, bl : bl + SUB, :]
        )

    def section(k, x0, rows):
        slot = k % 2
        new_slot = (k + 1) % 2

        def body(i, c):
            x = x0 + i
            for b in range(LB):
                lv = PAD + b * SUB
                bl = b * SUB
                halo = jnp.where(
                    odd, tcol_rx[k, 0, bl : bl + SUB, :], tcol_rx[k, 1, bl : bl + SUB, :]
                )
                edge = roll(halo, back(x))
                center = T[slot, x + 1, lv : lv + SUB, :]
                north = roll(jnp.where(first, edge, center), LANES - 1)
                south = roll(jnp.where(last, edge, center), 1)
                east = T[slot, x + 2, lv : lv + SUB, :]
                west = T[slot, x, lv : lv + SUB, :]
                upper = T[slot, x + 1, lv + 1 : lv + 1 + SUB, :]
                lower = T[slot, x + 1, lv - 1 : lv - 1 + SUB, :]
                u = U[SWEEPS % 2, 0, x + 1, lv : lv + SUB, :]
                v = U[SWEEPS % 2, 1, x + 1, lv : lv + SUB, :]
                advect = (
                    jnp.maximum(u, 0.0) * (center - west)
                    + jnp.minimum(u, 0.0) * (east - center)
                    + jnp.maximum(v, 0.0) * (center - south)
                    + jnp.minimum(v, 0.0) * (north - center)
                )
                value = (
                    center
                    + 0.1 * (east + west + north + south - 4.0 * center)
                    + 0.2 * (upper + lower - 2.0 * center)
                    - 0.05 * advect
                    + Q[0, x, bl : bl + SUB, :]
                )
                if k < SECTIONS - 1:
                    put_theta(new_slot, k + 1, x, b, value)
                else:
                    place = pl.ds(bl * R + x, SUB, stride=R)
                    warm_flat[place, :] = value
                    hard_flat[place, :] = jnp.exp(-0.6 * value)
            return c

        lax.fori_loop(0, rows, body, 0)

    vel_flat = [vel_st.at[f].reshape(L * R, LANES) for f in range(2)]
    rate_flat = rate_st.reshape(L * R, LANES)
    warm_flat = warm_st.reshape(L * R, LANES)
    hard_flat = hard_st.reshape(L * R, LANES)

    for cp in vel_cp:
        cp.wait()

    def load_vel(x, c):
        for b in range(LB):
            place = pl.ds(b * SUB * R + x, SUB, stride=R)
            put_vel(0, 0, x, b, (vel_flat[0][place, :], vel_flat[1][place, :]))
        return c

    pk[...] = jnp.zeros_like(pk)
    tpk[...] = jnp.zeros_like(tpk)
    lax.fori_loop(0, R, load_vel, 0)
    put_diag(0, 0)
    start(vel_moves(0), vs_sem.at[0], vr_sem.at[0])
    warm = [warm_copy(d) for d in range(m)]
    for cp in warm:
        cp.start()
    rate_cp.wait()

    def load_rate(x, c):
        for b in range(LB):
            place = pl.ds(b * SUB * R + x, SUB, stride=R)
            Q[1, x, b * SUB : (b + 1) * SUB, :] = rate_flat[place, :]
        return c

    lax.fori_loop(0, R, load_rate, 0)

    for k in range(SWEEPS):
        finish(vel_moves(k), vs_sem.at[k], vr_sem.at[k])
        prepare(k)
        sweep(k)
        if k + 1 < SWEEPS:
            put_diag((k + 1) % 2, k + 1)
        start(vel_moves(k + 1), vs_sem.at[k + 1], vr_sem.at[k + 1])
        if k == 1:
            for cp in warm:
                cp.wait()
            for slot in range(2):
                for x in range(R + 2):
                    T[slot, x, PAD - 1 : PAD, :] = jnp.zeros((1, LANES), f32)
                    T[slot, x, PAD + L : PAD + L + 1, :] = jnp.zeros((1, LANES), f32)

            def load_warm(x, c):
                for b in range(LB):
                    place = pl.ds(b * SUB * R + x, SUB, stride=R)
                    put_theta(0, 0, x, b, warm_flat[place, :])
                return c

            lax.fori_loop(0, R, load_warm, 0)
            start(th_moves(0), ts_sem.at[0], tr_sem.at[0])

    vel_back = [
        pltpu.make_async_copy(vel_st.at[f], vel_out.at[f], loc_sem.at[f]) for f in range(2)
    ]
    for cp in vel_back:
        cp.start()

    finish(vel_moves(SWEEPS), vs_sem.at[SWEEPS], vr_sem.at[SWEEPS])
    prepare(SWEEPS)

    def heat_body(x, c):
        ice = icy[pl.ds(x, 1), :].astype(f32)
        for b in range(LB):
            bl = b * SUB
            effective, visc = strain(SWEEPS % 2, x, b)[:2]
            Q[0, x, bl : bl + SUB, :] = (ice * 0.1) * visc * effective
        return c

    lax.fori_loop(0, R, heat_body, 0)

    outs = []
    for k in range(SECTIONS):
        finish(th_moves(k), ts_sem.at[k], tr_sem.at[k])
        for side, row in ((0, 0), (1, R + 1)):
            T[k % 2, row, PAD : PAD + L, :] = trow_rx[k, side]
        if k < SECTIONS - 1:
            section(k, 0, R)
            start(th_moves(k + 1), ts_sem.at[k + 1], tr_sem.at[k + 1])
            continue
        for c in range(R // SUB):
            section(k, c * SUB, SUB)
            for d in list(range(1, m)) + [0]:
                to = lax.rem(g + d, m)
                src = warm_st.at[pl.ds(to * LG, LG), c * SUB : (c + 1) * SUB, :]
                dst = temp_out.at[
                    :,
                    c * SUB : (c + 1) * SUB,
                    pl.ds(pl.multiple_of(g * LANES, LANES), LANES),
                ]
                if d == 0:
                    cp = pltpu.make_async_copy(src, dst, os_sem.at[c, 0])
                else:
                    cp = pltpu.make_async_remote_copy(
                        src,
                        dst,
                        os_sem.at[c, d],
                        or_sem.at[c, d],
                        device_id=(t, to),
                        device_id_type=MESH,
                    )
                cp.start()
                outs.append(cp)
    hard_back = pltpu.make_async_copy(hard_st, hard_out, loc_sem.at[2])
    hard_back.start()
    for cp in outs:
        cp.wait()
    for cp in vel_back:
        cp.wait()
    hard_back.wait()


def local(n, m, vel, rate, warm, grav, slide, icy, bed):
    _, L, R, Y = vel.shape
    LG = L // m
    assert Y == LANES and 4 * R <= LANES and R % SUB == 0 and L % (SUB * m) == 0
    f32 = jnp.float32
    any_spec = pl.BlockSpec(memory_space=pl.ANY)
    vmem = pl.BlockSpec(memory_space=pltpu.VMEM)
    K = SWEEPS + 1
    V = pltpu.VMEM
    dma = pltpu.SemaphoreType.DMA
    return pl.pallas_call(
        functools.partial(kernel, n, m, R, L, LG),
        out_shape=(
            jax.ShapeDtypeStruct(vel.shape, f32),
            jax.ShapeDtypeStruct(warm.shape, f32),
            jax.ShapeDtypeStruct(rate.shape, f32),
        ),
        in_specs=[any_spec] * 3 + [vmem] * 4,
        out_specs=(any_spec,) * 3,
        scratch_shapes=[
            V((2, L, R, LANES), f32),
            V((L, R, LANES), f32),
            V((L, R, LANES), f32),
            V((L, R, LANES), f32),
            V((2, 2, R + 2, L + 2 * PAD, LANES), f32),
            V((2, R + 2, L, LANES), f32),
            V((2, R, L, LANES), f32),
            V((2, R + 2, L + 2 * PAD, LANES), f32),
            V((2, R, L, LANES), f32),
            V((K, L, LANES), f32),
            V((SWEEPS, 2, SUB, LANES), f32),
            V((K, 2, 2, L, LANES), f32),
            V((K, 2, L, LANES), f32),
            V((SWEEPS, 2, 2, SUB, LANES), f32),
            V((SECTIONS, L, LANES), f32),
            V((SECTIONS, 2, L, LANES), f32),
            V((SECTIONS, 2, L, LANES), f32),
            dma((4,)),
            dma((K, 8)),
            dma((K, 8)),
            dma((SECTIONS, 4)),
            dma((SECTIONS, 4)),
            dma((m,)),
            dma((m,)),
            dma((R // SUB, m)),
            dma((R // SUB, m)),
        ],
        compiler_params=pltpu.CompilerParams(
            collective_id=0, has_side_effects=True, vmem_limit_bytes=48 * 1024 * 1024
        ),
        name="ice_step",
    )(vel, rate, warm, grav, slide, icy, bed)


def solution(mesh):
    return jax.shard_map(
        functools.partial(local, mesh.shape["tile"], mesh.shape["grp"]),
        mesh=mesh,
        in_specs=(
            P(None, None, "tile", "grp"),
            P(None, "tile", "grp"),
            P("grp", "tile", None),
            P(None, "tile", "grp"),
            P("tile", "grp"),
            P("tile", "grp"),
            P("tile", "grp"),
        ),
        out_specs=(P(None, None, "tile", "grp"), P("grp", "tile", None), P(None, "tile", "grp")),
        check_vma=False,
    )
```

```python
import functools

import jax
import jax.numpy as jnp
from jax import lax
from jax.experimental import pallas as pl
from jax.experimental.pallas import tpu as pltpu
from jax.sharding import PartitionSpec as P

SWEEPS = 4
SECTIONS = 4
LANES = 128
SUB = 8
PAD = 8

MESH = pl.DeviceIdType.MESH


def roll(x, shift, axis=1):
    return pltpu.roll(x, shift, axis)


def kernel(
    n,
    m,
    R,
    L,
    LG,
    vel_in,
    rate_in,
    warm_in,
    grav,
    slide,
    icy,
    bed,
    vel_out,
    temp_out,
    hard_out,
    vel_st,
    rate_st,
    warm_st,
    hard_st,
    U0,
    U1,
    DY,
    SY,
    T0,
    T1,
    mh,
    tmh,
    Q,
    pk,
    dk,
    row_rx,
    col_rx,
    diag_rx,
    tpk,
    trow_rx,
    tcol_rx,
    loc_sem,
    vs_sem,
    vr_sem,
    ts_sem,
    tr_sem,
    ws_sem,
    wr_sem,
    os_sem,
    or_sem,
):
    t = lax.axis_index("tile")
    g = lax.axis_index("grp")
    LB = L // SUB
    U = (U0, U1)
    T = (T0, T1)
    STEP = 2
    f32 = jnp.float32

    vel_cp = [
        pltpu.make_async_copy(vel_in.at[f], vel_st.at[f], loc_sem.at[f]) for f in range(2)
    ]
    rate_cp = pltpu.make_async_copy(rate_in, rate_st, loc_sem.at[2])
    for cp in vel_cp:
        cp.start()
    rate_cp.start()

    lo_t, hi_t, lo_g, hi_g = t > 0, t < n - 1, g > 0, g < m - 1

    def has(dt, dg):
        ok = None
        for d, lo, hi in ((dt, lo_t, hi_t), (dg, lo_g, hi_g)):
            if d:
                c = lo if d < 0 else hi
                ok = c if ok is None else jnp.logical_and(ok, c)
        return ok

    for ref in (row_rx, col_rx, diag_rx, trow_rx, tcol_rx):
        ref[...] = jnp.zeros_like(ref)

    barrier = pltpu.get_barrier_semaphore()
    around = [(-1, -1), (-1, 0), (-1, 1), (1, -1), (1, 0), (1, 1)]
    for dt, dg in around:

        @pl.when(has(dt, dg))
        def _(dt=dt, dg=dg):
            pl.semaphore_signal(
                barrier, inc=1, device_id=(t + dt, g + dg), device_id_type=MESH
            )

    for d in range(1, m):
        pl.semaphore_signal(
            barrier, inc=1, device_id=(t, lax.rem(g + d, m)), device_id_type=MESH
        )

    sides_t = lo_t.astype(jnp.int32) + hi_t.astype(jnp.int32)
    sides_g = lo_g.astype(jnp.int32) + hi_g.astype(jnp.int32)
    pl.semaphore_wait(barrier, m - 1 + sides_t * (1 + sides_g))

    def warm_copy(d):
        to = lax.rem(g + d, m)
        src = warm_in.at[:, :, pl.ds(pl.multiple_of(to * LANES, LANES), LANES)]
        dst = warm_st.at[pl.ds(g * LG, LG)]
        if d == 0:
            return pltpu.make_async_copy(src, dst, loc_sem.at[3])
        return pltpu.make_async_remote_copy(
            src, dst, ws_sem.at[d], wr_sem.at[d], device_id=(t, to), device_id_type=MESH
        )

    lane = lax.broadcasted_iota(jnp.int32, (SUB, LANES), 1)
    subl = lax.broadcasted_iota(jnp.int32, (SUB, LANES), 0)
    first = lane == 0
    last = lane == LANES - 1
    odd = lax.rem(lane, 2) == 1
    half = LANES // 2
    u_edge = jnp.logical_or(first, last)

    def back(x, extra=0):
        return lax.rem(2 * LANES - 1 - 2 * x - extra, LANES)

    def near_lane(x, shift):
        lane_x = lax.rem(lane + (LANES + 1) - shift, LANES)
        return lane_x < 2

    def vel_moves(k):
        slot = k % 2
        moves = [
            ((1, 0), U[slot].at[:, R, PAD : PAD + L, :], row_rx.at[k, 0]),
            ((-1, 0), U[slot].at[:, 1, PAD : PAD + L, :], row_rx.at[k, 1]),
            ((0, 1), pk.at[k], col_rx.at[k, 0]),
            ((0, -1), pk.at[k], col_rx.at[k, 1]),
        ]
        if k < SWEEPS:
            moves += [
                ((1, 1), dk.at[k, 1], diag_rx.at[k, 0, 0]),
                ((1, -1), dk.at[k, 1], diag_rx.at[k, 0, 1]),
                ((-1, 1), dk.at[k, 0], diag_rx.at[k, 1, 0]),
                ((-1, -1), dk.at[k, 0], diag_rx.at[k, 1, 1]),
            ]
        return moves

    def start(moves, s_sem, r_sem):
        for j, ((dt, dg), src, dst) in enumerate(moves):

            @pl.when(has(dt, dg))
            def _(j=j, dt=dt, dg=dg, src=src, dst=dst):
                pltpu.make_async_remote_copy(
                    src,
                    dst,
                    s_sem.at[j],
                    r_sem.at[j],
                    device_id=(t + dt, g + dg),
                    device_id_type=MESH,
                ).start()

    def finish(moves, s_sem, r_sem):
        for j, ((dt, dg), src, dst) in enumerate(moves):

            @pl.when(has(dt, dg))
            def _(j=j, dt=dt, dg=dg, src=src, dst=dst):
                pltpu.make_async_remote_copy(
                    src,
                    dst,
                    s_sem.at[j],
                    r_sem.at[j],
                    device_id=(t + dt, g + dg),
                    device_id_type=MESH,
                ).wait_send()

            @pl.when(has(-dt, -dg))
            def _(j=j, dt=dt, dg=dg, src=src, dst=dst):
                pltpu.make_async_remote_copy(
                    src,
                    dst,
                    s_sem.at[j],
                    r_sem.at[j],
                    device_id=(t - dt, g - dg),
                    device_id_type=MESH,
                ).wait_recv()

    def put_vel(slot, k, x, b, values):
        lv = PAD + b * SUB
        for f in range(2):
            U[slot][f, x + 1, lv : lv + SUB, :] = values[f]
            if b == 0:
                U[slot][f, x + 1, lv - 1 : lv, :] = values[f][0:1]
            if b == LB - 1:
                U[slot][f, x + 1, lv + SUB : lv + SUB + 1, :] = values[f][SUB - 1 : SUB]
        bl = b * SUB
        w = jnp.where(
            near_lane(x, 2 * x + half),
            roll(values[1], lax.rem(2 * x + half, LANES)),
            pk[k, bl : bl + SUB, :],
        )
        pk[k, bl : bl + SUB, :] = jnp.where(near_lane(x, 2 * x), roll(values[0], 2 * x), w)

    def put_diag(slot, k):
        for side, x in ((0, 1), (1, R)):
            acc = jnp.zeros((SUB, LANES), f32)
            for b in range(LB):
                lv = PAD + b * SUB
                u = U[slot][0, x, lv : lv + SUB, :]
                v = U[slot][1, x, lv : lv + SUB, :]
                w = jnp.where(u_edge, u, roll(v, half))
                w = roll(w, 2 * b) if b else w
                hit = jnp.logical_or(near_lane(b, 2 * b), near_lane(b, 2 * b + half))
                acc = jnp.where(hit, w, acc)
            dk[k, side] = acc

    def fill_level_pads(slot, row):
        for f in range(2):
            U[slot][f, row, PAD - 1 : PAD, :] = U[slot][f, row, PAD : PAD + 1, :]
            U[slot][f, row, PAD + L : PAD + L + 1, :] = U[slot][
                f, row, PAD + L - 1 : PAD + L, :
            ]

    def lane_parts(f, row, b, u, edge):
        up = jnp.where(last, edge, roll(u, LANES - 1))
        down = jnp.where(first, edge, roll(u, 1))
        bl = b * SUB
        DY[f, row, bl : bl + SUB, :] = up - down
        return up + down, bl

    def prepare(k):
        slot = k % 2
        for side, row in ((0, 0), (1, R + 1)):
            for f in range(2):
                U[slot][f, row, PAD : PAD + L, :] = row_rx[k, side, f]
            if k < SWEEPS:
                corner = jnp.where(odd, roll(diag_rx[k, side, 0], 2), diag_rx[k, side, 1])
                for b in range(LB):
                    lv = PAD + b * SUB
                    for f in range(2):
                        edge = roll(corner, (2 * LANES - 2 * b - 1 - f * half) % LANES)
                        lane_parts(f, row, b, U[slot][f, row, lv : lv + SUB, :], edge)

        for b in range(LB):
            bl = b * SUB
            mh[bl : bl + SUB, :] = jnp.where(
                odd, roll(col_rx[k, 0, bl : bl + SUB, :], 2), col_rx[k, 1, bl : bl + SUB, :]
            )

        def body(i, c):
            for b in range(LB):
                lv = PAD + b * SUB
                bl = b * SUB
                halo = mh[bl : bl + SUB, :]
                for x in [i * STEP + j for j in range(STEP)]:
                    for f in range(2):
                        edge = roll(halo, back(x, f * half))
                        u = U[slot][f, x + 1, lv : lv + SUB, :]
                        s, _ = lane_parts(f, x + 1, b, u, edge)
                        if k < SWEEPS:
                            SY[f, x, bl : bl + SUB, :] = s
            return c

        lax.fori_loop(0, R // STEP, body, 0)

    def strain(slot, x, b):
        lv = PAD + b * SUB
        bl = b * SUB
        ue = U[slot][0, x + 2, lv : lv + SUB, :]
        uw = U[slot][0, x, lv : lv + SUB, :]
        ve = U[slot][1, x + 2, lv : lv + SUB, :]
        vw = U[slot][1, x, lv : lv + SUB, :]
        uu = U[slot][0, x + 1, lv + 1 : lv + 1 + SUB, :]
        ul = U[slot][0, x + 1, lv - 1 : lv - 1 + SUB, :]
        vu = U[slot][1, x + 1, lv + 1 : lv + 1 + SUB, :]
        vl = U[slot][1, x + 1, lv - 1 : lv - 1 + SUB, :]
        dyu = DY[0, x + 1, bl : bl + SUB, :]
        dyv = DY[1, x + 1, bl : bl + SUB, :]
        xx = ue - uw
        shear = dyu + (ve - vw)
        du = uu - ul
        dv = vu - vl
        effective = 0.25 * (
            xx * xx + dyv * dyv + xx * dyv + 0.25 * (shear * shear + du * du + dv * dv)
        )
        rate = Q[1, x, bl : bl + SUB, :]
        viscosity = rate * jnp.exp(jnp.log(effective + 0.01) * (-1.0 / 3.0))
        return effective, viscosity, ue + uw, ve + vw, uu + ul, vu + vl

    def sweep(k):
        slot = k % 2
        new_slot = (k + 1) % 2

        def row(x):
            ice = icy[pl.ds(x, 1), :].astype(f32)
            drag = slide[pl.ds(x, 1), :] * bed[pl.ds(x, 1), :].astype(f32)
            water = 1.0 - ice
            gu = grav[0, pl.ds(x, 1), :]
            gv = grav[1, pl.ds(x, 1), :]
            for b in range(LB):
                bl = b * SUB
                _, visc, sxu, sxv, szu, szv = strain(slot, x, b)
                diagonal = 22.0 * visc + water
                if b == 0:
                    diagonal = diagonal + jnp.where(subl == 0, drag, 0.0)
                cross_u = DY[1, x + 2, bl : bl + SUB, :] - DY[1, x, bl : bl + SUB, :]
                cross_v = DY[0, x + 2, bl : bl + SUB, :] - DY[0, x, bl : bl + SUB, :]
                near_u = 4.0 * (sxu + szu) + SY[0, x, bl : bl + SUB, :] + 0.75 * cross_u
                near_v = (
                    sxv + 4.0 * (SY[1, x, bl : bl + SUB, :] + szv) + 0.75 * cross_v
                )
                scale = ice / diagonal
                new_u = (gu + visc * near_u) * scale
                new_v = (gv + visc * near_v) * scale
                put_vel(new_slot, k + 1, x, b, (new_u, new_v))
                if k == SWEEPS - 1:
                    place = pl.ds(bl * R + x, SUB, stride=R)
                    vel_flat[0][place, :] = new_u
                    vel_flat[1][place, :] = new_v

        def body(i, c):
            for j in range(STEP):
                row(i * STEP + j)
            return c

        lax.fori_loop(0, R // STEP, body, 0)

    def th_moves(k):
        slot = k % 2
        return [
            ((1, 0), T[slot].at[R, PAD : PAD + L, :], trow_rx.at[k, 0]),
            ((-1, 0), T[slot].at[1, PAD : PAD + L, :], trow_rx.at[k, 1]),
            ((0, 1), tpk.at[k], tcol_rx.at[k, 0]),
            ((0, -1), tpk.at[k], tcol_rx.at[k, 1]),
        ]

    def put_theta(slot, k, x, b, value):
        lv = PAD + b * SUB
        bl = b * SUB
        T[slot][x + 1, lv : lv + SUB, :] = value
        w = roll(value, 2 * x)
        tpk[k, bl : bl + SUB, :] = jnp.where(
            near_lane(x, 2 * x), w, tpk[k, bl : bl + SUB, :]
        )

    def section(k, x0, rows):
        slot = k % 2
        new_slot = (k + 1) % 2

        def row(x):
            for b in range(LB):
                lv = PAD + b * SUB
                bl = b * SUB
                edge = roll(tmh[bl : bl + SUB, :], back(x))
                center = T[slot][x + 1, lv : lv + SUB, :]
                north = jnp.where(last, edge, roll(center, LANES - 1))
                south = jnp.where(first, edge, roll(center, 1))
                east = T[slot][x + 2, lv : lv + SUB, :]
                west = T[slot][x, lv : lv + SUB, :]
                upper = T[slot][x + 1, lv + 1 : lv + 1 + SUB, :]
                lower = T[slot][x + 1, lv - 1 : lv - 1 + SUB, :]
                u = U[SWEEPS % 2][0, x + 1, lv : lv + SUB, :]
                v = U[SWEEPS % 2][1, x + 1, lv : lv + SUB, :]
                advect = (
                    jnp.maximum(u, 0.0) * (center - west)
                    + jnp.minimum(u, 0.0) * (east - center)
                    + jnp.maximum(v, 0.0) * (center - south)
                    + jnp.minimum(v, 0.0) * (north - center)
                )
                value = (
                    center
                    + 0.1 * (east + west + north + south - 4.0 * center)
                    + 0.2 * (upper + lower - 2.0 * center)
                    - 0.05 * advect
                    + Q[0, x, bl : bl + SUB, :]
                )
                if k < SECTIONS - 1:
                    put_theta(new_slot, k + 1, x, b, value)
                else:
                    place = pl.ds(bl * R + x, SUB, stride=R)
                    warm_flat[place, :] = value
                    hard_flat[place, :] = jnp.exp(-0.6 * value)

        def body(i, c):
            for j in range(STEP):
                row(x0 + i * STEP + j)
            return c

        lax.fori_loop(0, rows // STEP, body, 0)

    vel_flat = [vel_st.at[f].reshape(L * R, LANES) for f in range(2)]
    rate_flat = rate_st.reshape(L * R, LANES)
    warm_flat = warm_st.reshape(L * R, LANES)
    hard_flat = hard_st.reshape(L * R, LANES)

    for cp in vel_cp:
        cp.wait()

    def load_vel(x, c):
        for b in range(LB):
            place = pl.ds(b * SUB * R + x, SUB, stride=R)
            put_vel(0, 0, x, b, (vel_flat[0][place, :], vel_flat[1][place, :]))
        return c

    pk[...] = jnp.zeros_like(pk)
    tpk[...] = jnp.zeros_like(tpk)
    lax.fori_loop(0, R, load_vel, 0)
    put_diag(0, 0)
    start(vel_moves(0), vs_sem.at[0], vr_sem.at[0])
    warm = [warm_copy(d) for d in range(m)]
    warm[0].start()
    rate_cp.wait()

    def load_rate(x, c):
        for b in range(LB):
            place = pl.ds(b * SUB * R + x, SUB, stride=R)
            Q[1, x, b * SUB : (b + 1) * SUB, :] = rate_flat[place, :]
        return c

    lax.fori_loop(0, R, load_rate, 0)

    for k in range(SWEEPS):
        finish(vel_moves(k), vs_sem.at[k], vr_sem.at[k])
        for cp in warm[1 + k :] if k == SWEEPS - 1 else warm[1 + k : 2 + k]:
            cp.start()
        prepare(k)
        sweep(k)
        if k + 1 < SWEEPS:
            put_diag((k + 1) % 2, k + 1)
        start(vel_moves(k + 1), vs_sem.at[k + 1], vr_sem.at[k + 1])
        if k == SWEEPS - 1:
            for cp in warm:
                cp.wait()
            for slot in range(2):
                for x in range(R + 2):
                    T[slot][x, PAD - 1 : PAD, :] = jnp.zeros((1, LANES), f32)
                    T[slot][x, PAD + L : PAD + L + 1, :] = jnp.zeros((1, LANES), f32)

            def load_warm(x, c):
                for b in range(LB):
                    place = pl.ds(b * SUB * R + x, SUB, stride=R)
                    put_theta(0, 0, x, b, warm_flat[place, :])
                return c

            lax.fori_loop(0, R, load_warm, 0)
            start(th_moves(0), ts_sem.at[0], tr_sem.at[0])

    vel_back = [
        pltpu.make_async_copy(vel_st.at[f], vel_out.at[f], loc_sem.at[f]) for f in range(2)
    ]
    for cp in vel_back:
        cp.start()

    finish(vel_moves(SWEEPS), vs_sem.at[SWEEPS], vr_sem.at[SWEEPS])
    prepare(SWEEPS)

    def heat_row(x):
        ice = icy[pl.ds(x, 1), :].astype(f32)
        for b in range(LB):
            bl = b * SUB
            effective, visc = strain(SWEEPS % 2, x, b)[:2]
            Q[0, x, bl : bl + SUB, :] = (ice * 0.1) * visc * effective

    def heat_body(i, c):
        for j in range(STEP):
            heat_row(i * STEP + j)
        return c

    lax.fori_loop(0, R // STEP, heat_body, 0)

    outs = []
    for k in range(SECTIONS):
        finish(th_moves(k), ts_sem.at[k], tr_sem.at[k])
        for side, row in ((0, 0), (1, R + 1)):
            T[k % 2][row, PAD : PAD + L, :] = trow_rx[k, side]
        for b in range(LB):
            bl = b * SUB
            tmh[bl : bl + SUB, :] = jnp.where(
                odd, roll(tcol_rx[k, 0, bl : bl + SUB, :], 2), tcol_rx[k, 1, bl : bl + SUB, :]
            )
        if k < SECTIONS - 1:
            section(k, 0, R)
            start(th_moves(k + 1), ts_sem.at[k + 1], tr_sem.at[k + 1])
            continue
        for c in range(R // SUB):
            section(k, c * SUB, SUB)
            for d in list(range(1, m)) + [0]:
                to = lax.rem(g + d, m)
                src = warm_st.at[pl.ds(to * LG, LG), c * SUB : (c + 1) * SUB, :]
                dst = temp_out.at[
                    :,
                    c * SUB : (c + 1) * SUB,
                    pl.ds(pl.multiple_of(g * LANES, LANES), LANES),
                ]
                if d == 0:
                    cp = pltpu.make_async_copy(src, dst, os_sem.at[c, 0])
                else:
                    cp = pltpu.make_async_remote_copy(
                        src,
                        dst,
                        os_sem.at[c, d],
                        or_sem.at[c, d],
                        device_id=(t, to),
                        device_id_type=MESH,
                    )
                cp.start()
                outs.append(cp)
    hard_back = pltpu.make_async_copy(hard_st, hard_out, loc_sem.at[2])
    hard_back.start()
    for cp in outs:
        cp.wait()
    for cp in vel_back:
        cp.wait()
    hard_back.wait()


def local(n, m, vel, rate, warm, grav, slide, icy, bed):
    _, L, R, Y = vel.shape
    LG = L // m
    assert Y == LANES and 4 * R <= LANES and R % SUB == 0 and L % (SUB * m) == 0
    f32 = jnp.float32
    any_spec = pl.BlockSpec(memory_space=pl.ANY)
    vmem = pl.BlockSpec(memory_space=pltpu.VMEM)
    K = SWEEPS + 1
    V = pltpu.VMEM
    dma = pltpu.SemaphoreType.DMA
    return pl.pallas_call(
        functools.partial(kernel, n, m, R, L, LG),
        out_shape=(
            jax.ShapeDtypeStruct(vel.shape, f32),
            jax.ShapeDtypeStruct(warm.shape, f32),
            jax.ShapeDtypeStruct(rate.shape, f32),
        ),
        in_specs=[any_spec] * 3 + [vmem] * 4,
        out_specs=(any_spec,) * 3,
        scratch_shapes=[
            V((2, L, R, LANES), f32),
            V((L, R, LANES), f32),
            V((L, R, LANES), f32),
            V((L, R, LANES), f32),
            V((2, R + 2, L + 2 * PAD, LANES), f32),
            V((2, R + 2, L + 2 * PAD, LANES), f32),
            V((2, R + 2, L, LANES), f32),
            V((2, R, L, LANES), f32),
            V((R + 2, L + 2 * PAD, LANES), f32),
            V((R + 2, L + 2 * PAD, LANES), f32),
            V((L, LANES), f32),
            V((L, LANES), f32),
            V((2, R, L, LANES), f32),
            V((K, L, LANES), f32),
            V((SWEEPS, 2, SUB, LANES), f32),
            V((K, 2, 2, L, LANES), f32),
            V((K, 2, L, LANES), f32),
            V((SWEEPS, 2, 2, SUB, LANES), f32),
            V((SECTIONS, L, LANES), f32),
            V((SECTIONS, 2, L, LANES), f32),
            V((SECTIONS, 2, L, LANES), f32),
            dma((4,)),
            dma((K, 8)),
            dma((K, 8)),
            dma((SECTIONS, 4)),
            dma((SECTIONS, 4)),
            dma((m,)),
            dma((m,)),
            dma((R // SUB, m)),
            dma((R // SUB, m)),
        ],
        compiler_params=pltpu.CompilerParams(
            collective_id=0, has_side_effects=True, vmem_limit_bytes=48 * 1024 * 1024
        ),
        name="ice_step",
    )(vel, rate, warm, grav, slide, icy, bed)


def solution(mesh):
    return jax.shard_map(
        functools.partial(local, mesh.shape["tile"], mesh.shape["grp"]),
        mesh=mesh,
        in_specs=(
            P(None, None, "tile", "grp"),
            P(None, "tile", "grp"),
            P("grp", "tile", None),
            P(None, "tile", "grp"),
            P("tile", "grp"),
            P("tile", "grp"),
            P("tile", "grp"),
        ),
        out_specs=(P(None, None, "tile", "grp"), P("grp", "tile", None), P(None, "tile", "grp")),
        check_vma=False,
    )
```

```python
import functools

import jax
import jax.numpy as jnp
from jax import lax
from jax.experimental import pallas as pl
from jax.experimental.pallas import tpu as pltpu
from jax.sharding import PartitionSpec as P

SWEEPS = 4
SECTIONS = 4
LANES = 128
SUB = 8
PAD = 8

MESH = pl.DeviceIdType.MESH


def roll(x, shift, axis=1):
    return pltpu.roll(x, shift, axis)


def kernel(
    n,
    m,
    R,
    L,
    LG,
    vel_in,
    rate_in,
    warm_in,
    grav,
    slide,
    icy,
    bed,
    vel_out,
    temp_out,
    hard_out,
    vel_st,
    rate_st,
    warm_st,
    hard_st,
    U0,
    U1,
    DY,
    SY,
    T0,
    T1,
    mh,
    tmh,
    Q,
    pk,
    dk,
    row_rx,
    col_rx,
    diag_rx,
    tpk,
    trow_rx,
    tcol_rx,
    loc_sem,
    vs_sem,
    vr_sem,
    ts_sem,
    tr_sem,
    ws_sem,
    wr_sem,
    os_sem,
    or_sem,
):
    t = lax.axis_index("tile")
    g = lax.axis_index("grp")
    LB = L // SUB
    U = (U0, U1)
    T = (T0, T1)
    STEP = 2
    f32 = jnp.float32

    vel_cp = [
        pltpu.make_async_copy(vel_in.at[f], vel_st.at[f], loc_sem.at[f]) for f in range(2)
    ]
    rate_cp = pltpu.make_async_copy(rate_in, rate_st, loc_sem.at[2])
    for cp in vel_cp:
        cp.start()
    rate_cp.start()

    lo_t, hi_t, lo_g, hi_g = t > 0, t < n - 1, g > 0, g < m - 1

    def has(dt, dg):
        ok = None
        for d, lo, hi in ((dt, lo_t, hi_t), (dg, lo_g, hi_g)):
            if d:
                c = lo if d < 0 else hi
                ok = c if ok is None else jnp.logical_and(ok, c)
        return ok

    for ref in (row_rx, col_rx, diag_rx, trow_rx, tcol_rx):
        ref[...] = jnp.zeros_like(ref)

    barrier = pltpu.get_barrier_semaphore()
    around = [(-1, -1), (-1, 0), (-1, 1), (1, -1), (1, 0), (1, 1)]
    for dt, dg in around:

        @pl.when(has(dt, dg))
        def _(dt=dt, dg=dg):
            pl.semaphore_signal(
                barrier, inc=1, device_id=(t + dt, g + dg), device_id_type=MESH
            )

    for d in range(1, m):
        pl.semaphore_signal(
            barrier, inc=1, device_id=(t, lax.rem(g + d, m)), device_id_type=MESH
        )

    sides_t = lo_t.astype(jnp.int32) + hi_t.astype(jnp.int32)
    sides_g = lo_g.astype(jnp.int32) + hi_g.astype(jnp.int32)
    pl.semaphore_wait(barrier, m - 1 + sides_t * (1 + sides_g))

    def warm_copy(d):
        to = lax.rem(g + d, m)
        src = warm_in.at[:, :, pl.ds(pl.multiple_of(to * LANES, LANES), LANES)]
        dst = warm_st.at[pl.ds(g * LG, LG)]
        if d == 0:
            return pltpu.make_async_copy(src, dst, loc_sem.at[3])
        return pltpu.make_async_remote_copy(
            src, dst, ws_sem.at[d], wr_sem.at[d], device_id=(t, to), device_id_type=MESH
        )

    lane = lax.broadcasted_iota(jnp.int32, (SUB, LANES), 1)
    subl = lax.broadcasted_iota(jnp.int32, (SUB, LANES), 0)
    first = lane == 0
    last = lane == LANES - 1
    odd = lax.rem(lane, 2) == 1
    half = LANES // 2
    u_edge = jnp.logical_or(first, last)

    def back(x, extra=0):
        return lax.rem(2 * LANES - 1 - 2 * x - extra, LANES)

    def near_lane(x, shift):
        lane_x = lax.rem(lane + (LANES + 1) - shift, LANES)
        return lane_x < 2

    def vel_moves(k):
        slot = k % 2
        moves = [
            ((1, 0), U[slot].at[:, R, PAD : PAD + L, :], row_rx.at[k, 0]),
            ((-1, 0), U[slot].at[:, 1, PAD : PAD + L, :], row_rx.at[k, 1]),
            ((0, 1), pk.at[k], col_rx.at[k, 0]),
            ((0, -1), pk.at[k], col_rx.at[k, 1]),
        ]
        if k < SWEEPS:
            moves += [
                ((1, 1), dk.at[k, 1], diag_rx.at[k, 0, 0]),
                ((1, -1), dk.at[k, 1], diag_rx.at[k, 0, 1]),
                ((-1, 1), dk.at[k, 0], diag_rx.at[k, 1, 0]),
                ((-1, -1), dk.at[k, 0], diag_rx.at[k, 1, 1]),
            ]
        return moves

    def start(moves, s_sem, r_sem, early=None):
        for j, ((dt, dg), src, dst) in enumerate(moves):
            if early is not None and early != (dt != 0):
                continue

            @pl.when(has(dt, dg))
            def _(j=j, dt=dt, dg=dg, src=src, dst=dst):
                pltpu.make_async_remote_copy(
                    src,
                    dst,
                    s_sem.at[j],
                    r_sem.at[j],
                    device_id=(t + dt, g + dg),
                    device_id_type=MESH,
                ).start()

    def finish(moves, s_sem, r_sem):
        for j, ((dt, dg), src, dst) in enumerate(moves):

            @pl.when(has(dt, dg))
            def _(j=j, dt=dt, dg=dg, src=src, dst=dst):
                pltpu.make_async_remote_copy(
                    src,
                    dst,
                    s_sem.at[j],
                    r_sem.at[j],
                    device_id=(t + dt, g + dg),
                    device_id_type=MESH,
                ).wait_send()

            @pl.when(has(-dt, -dg))
            def _(j=j, dt=dt, dg=dg, src=src, dst=dst):
                pltpu.make_async_remote_copy(
                    src,
                    dst,
                    s_sem.at[j],
                    r_sem.at[j],
                    device_id=(t - dt, g - dg),
                    device_id_type=MESH,
                ).wait_recv()

    def put_vel(slot, k, x, b, values):
        lv = PAD + b * SUB
        for f in range(2):
            U[slot][f, x + 1, lv : lv + SUB, :] = values[f]
            if b == 0:
                U[slot][f, x + 1, lv - 1 : lv, :] = values[f][0:1]
            if b == LB - 1:
                U[slot][f, x + 1, lv + SUB : lv + SUB + 1, :] = values[f][SUB - 1 : SUB]
        bl = b * SUB
        w = jnp.where(
            near_lane(x, 2 * x + half),
            roll(values[1], lax.rem(2 * x + half, LANES)),
            pk[k, bl : bl + SUB, :],
        )
        pk[k, bl : bl + SUB, :] = jnp.where(near_lane(x, 2 * x), roll(values[0], 2 * x), w)

    def put_diag(slot, k):
        for side, x in ((0, 1), (1, R)):
            acc = jnp.zeros((SUB, LANES), f32)
            for b in range(LB):
                lv = PAD + b * SUB
                u = U[slot][0, x, lv : lv + SUB, :]
                v = U[slot][1, x, lv : lv + SUB, :]
                w = jnp.where(u_edge, u, roll(v, half))
                w = roll(w, 2 * b) if b else w
                hit = jnp.logical_or(near_lane(b, 2 * b), near_lane(b, 2 * b + half))
                acc = jnp.where(hit, w, acc)
            dk[k, side] = acc

    def fill_level_pads(slot, row):
        for f in range(2):
            U[slot][f, row, PAD - 1 : PAD, :] = U[slot][f, row, PAD : PAD + 1, :]
            U[slot][f, row, PAD + L : PAD + L + 1, :] = U[slot][
                f, row, PAD + L - 1 : PAD + L, :
            ]

    def lane_parts(f, row, b, u, edge):
        up = jnp.where(last, edge, roll(u, LANES - 1))
        down = jnp.where(first, edge, roll(u, 1))
        bl = b * SUB
        DY[f, row, bl : bl + SUB, :] = up - down
        return up + down, bl

    def prepare(k):
        slot = k % 2
        for side, row in ((0, 0), (1, R + 1)):
            for f in range(2):
                U[slot][f, row, PAD : PAD + L, :] = row_rx[k, side, f]
            if k < SWEEPS:
                corner = jnp.where(odd, roll(diag_rx[k, side, 0], 2), diag_rx[k, side, 1])
                for b in range(LB):
                    lv = PAD + b * SUB
                    for f in range(2):
                        edge = roll(corner, (2 * LANES - 2 * b - 1 - f * half) % LANES)
                        lane_parts(f, row, b, U[slot][f, row, lv : lv + SUB, :], edge)

        for b in range(LB):
            bl = b * SUB
            mh[bl : bl + SUB, :] = jnp.where(
                odd, roll(col_rx[k, 0, bl : bl + SUB, :], 2), col_rx[k, 1, bl : bl + SUB, :]
            )

        def body(i, c):
            for b in range(LB):
                lv = PAD + b * SUB
                bl = b * SUB
                halo = mh[bl : bl + SUB, :]
                for x in [i * STEP + j for j in range(STEP)]:
                    for f in range(2):
                        edge = roll(halo, back(x, f * half))
                        u = U[slot][f, x + 1, lv : lv + SUB, :]
                        s, _ = lane_parts(f, x + 1, b, u, edge)
                        if k < SWEEPS:
                            SY[f, x, bl : bl + SUB, :] = s
            return c

        lax.fori_loop(0, R // STEP, body, 0)

    def strain(slot, x, b):
        lv = PAD + b * SUB
        bl = b * SUB
        ue = U[slot][0, x + 2, lv : lv + SUB, :]
        uw = U[slot][0, x, lv : lv + SUB, :]
        ve = U[slot][1, x + 2, lv : lv + SUB, :]
        vw = U[slot][1, x, lv : lv + SUB, :]
        uu = U[slot][0, x + 1, lv + 1 : lv + 1 + SUB, :]
        ul = U[slot][0, x + 1, lv - 1 : lv - 1 + SUB, :]
        vu = U[slot][1, x + 1, lv + 1 : lv + 1 + SUB, :]
        vl = U[slot][1, x + 1, lv - 1 : lv - 1 + SUB, :]
        dyu = DY[0, x + 1, bl : bl + SUB, :]
        dyv = DY[1, x + 1, bl : bl + SUB, :]
        xx = ue - uw
        shear = dyu + (ve - vw)
        du = uu - ul
        dv = vu - vl
        effective = 0.25 * (
            xx * xx + dyv * dyv + xx * dyv + 0.25 * (shear * shear + du * du + dv * dv)
        )
        rate = Q[1, x, bl : bl + SUB, :]
        viscosity = rate * jnp.exp(jnp.log(effective + 0.01) * (-1.0 / 3.0))
        return effective, viscosity, ue + uw, ve + vw, uu + ul, vu + vl

    def sweep(k):
        slot = k % 2
        new_slot = (k + 1) % 2

        def row(x):
            ice = icy[pl.ds(x, 1), :].astype(f32)
            drag = slide[pl.ds(x, 1), :] * bed[pl.ds(x, 1), :].astype(f32)
            water = 1.0 - ice
            gu = grav[0, pl.ds(x, 1), :]
            gv = grav[1, pl.ds(x, 1), :]
            for b in range(LB):
                bl = b * SUB
                _, visc, sxu, sxv, szu, szv = strain(slot, x, b)
                diagonal = 22.0 * visc + water
                if b == 0:
                    diagonal = diagonal + jnp.where(subl == 0, drag, 0.0)
                cross_u = DY[1, x + 2, bl : bl + SUB, :] - DY[1, x, bl : bl + SUB, :]
                cross_v = DY[0, x + 2, bl : bl + SUB, :] - DY[0, x, bl : bl + SUB, :]
                near_u = 4.0 * (sxu + szu) + SY[0, x, bl : bl + SUB, :] + 0.75 * cross_u
                near_v = (
                    sxv + 4.0 * (SY[1, x, bl : bl + SUB, :] + szv) + 0.75 * cross_v
                )
                scale = ice / diagonal
                new_u = (gu + visc * near_u) * scale
                new_v = (gv + visc * near_v) * scale
                put_vel(new_slot, k + 1, x, b, (new_u, new_v))
                if k == SWEEPS - 1:
                    place = pl.ds(bl * R + x, SUB, stride=R)
                    vel_flat[0][place, :] = new_u
                    vel_flat[1][place, :] = new_v

        def body(i, c):
            row(i)
            row(R - 1 - i)
            return c

        lax.fori_loop(0, 1, body, 0)
        if k + 1 < SWEEPS:
            put_diag(new_slot, k + 1)
        moves = vel_moves(k + 1), vs_sem.at[k + 1], vr_sem.at[k + 1]
        start(*moves, early=True)
        lax.fori_loop(1, R // 2, body, 0)
        start(*moves, early=False)

    def th_moves(k):
        slot = k % 2
        return [
            ((1, 0), T[slot].at[R, PAD : PAD + L, :], trow_rx.at[k, 0]),
            ((-1, 0), T[slot].at[1, PAD : PAD + L, :], trow_rx.at[k, 1]),
            ((0, 1), tpk.at[k], tcol_rx.at[k, 0]),
            ((0, -1), tpk.at[k], tcol_rx.at[k, 1]),
        ]

    def put_theta(slot, k, x, b, value):
        lv = PAD + b * SUB
        bl = b * SUB
        T[slot][x + 1, lv : lv + SUB, :] = value
        w = roll(value, 2 * x)
        tpk[k, bl : bl + SUB, :] = jnp.where(
            near_lane(x, 2 * x), w, tpk[k, bl : bl + SUB, :]
        )

    def section(k, x0, rows):
        slot = k % 2
        new_slot = (k + 1) % 2

        def row(x):
            for b in range(LB):
                lv = PAD + b * SUB
                bl = b * SUB
                edge = roll(tmh[bl : bl + SUB, :], back(x))
                center = T[slot][x + 1, lv : lv + SUB, :]
                north = jnp.where(last, edge, roll(center, LANES - 1))
                south = jnp.where(first, edge, roll(center, 1))
                east = T[slot][x + 2, lv : lv + SUB, :]
                west = T[slot][x, lv : lv + SUB, :]
                upper = T[slot][x + 1, lv + 1 : lv + 1 + SUB, :]
                lower = T[slot][x + 1, lv - 1 : lv - 1 + SUB, :]
                u = U[SWEEPS % 2][0, x + 1, lv : lv + SUB, :]
                v = U[SWEEPS % 2][1, x + 1, lv : lv + SUB, :]
                advect = (
                    jnp.maximum(u, 0.0) * (center - west)
                    + jnp.minimum(u, 0.0) * (east - center)
                    + jnp.maximum(v, 0.0) * (center - south)
                    + jnp.minimum(v, 0.0) * (north - center)
                )
                value = (
                    center
                    + 0.1 * (east + west + north + south - 4.0 * center)
                    + 0.2 * (upper + lower - 2.0 * center)
                    - 0.05 * advect
                    + Q[0, x, bl : bl + SUB, :]
                )
                if k < SECTIONS - 1:
                    put_theta(new_slot, k + 1, x, b, value)
                else:
                    place = pl.ds(bl * R + x, SUB, stride=R)
                    warm_flat[place, :] = value
                    hard_flat[place, :] = jnp.exp(-0.6 * value)

        if k == SECTIONS - 1:

            def chunk(i, c):
                for j in range(STEP):
                    row(x0 + i * STEP + j)
                return c

            lax.fori_loop(0, rows // STEP, chunk, 0)
            return

        def body(i, c):
            row(i)
            row(R - 1 - i)
            return c

        lax.fori_loop(0, 1, body, 0)
        moves = th_moves(k + 1), ts_sem.at[k + 1], tr_sem.at[k + 1]
        start(*moves, early=True)
        lax.fori_loop(1, R // 2, body, 0)
        start(*moves, early=False)

    vel_flat = [vel_st.at[f].reshape(L * R, LANES) for f in range(2)]
    rate_flat = rate_st.reshape(L * R, LANES)
    warm_flat = warm_st.reshape(L * R, LANES)
    hard_flat = hard_st.reshape(L * R, LANES)

    for cp in vel_cp:
        cp.wait()

    def load_vel(x, c):
        for b in range(LB):
            place = pl.ds(b * SUB * R + x, SUB, stride=R)
            put_vel(0, 0, x, b, (vel_flat[0][place, :], vel_flat[1][place, :]))
        return c

    pk[...] = jnp.zeros_like(pk)
    tpk[...] = jnp.zeros_like(tpk)
    lax.fori_loop(0, R, load_vel, 0)
    put_diag(0, 0)
    start(vel_moves(0), vs_sem.at[0], vr_sem.at[0])
    warm = [warm_copy(d) for d in range(m)]
    warm[0].start()
    rate_cp.wait()

    def load_rate(x, c):
        for b in range(LB):
            place = pl.ds(b * SUB * R + x, SUB, stride=R)
            Q[1, x, b * SUB : (b + 1) * SUB, :] = rate_flat[place, :]
        return c

    lax.fori_loop(0, R, load_rate, 0)

    for k in range(SWEEPS):
        finish(vel_moves(k), vs_sem.at[k], vr_sem.at[k])
        for cp in warm[1 + k :] if k == SWEEPS - 1 else warm[1 + k : 2 + k]:
            cp.start()
        prepare(k)
        sweep(k)
        if k == SWEEPS - 1:
            for cp in warm:
                cp.wait()
            for slot in range(2):
                for x in range(R + 2):
                    T[slot][x, PAD - 1 : PAD, :] = jnp.zeros((1, LANES), f32)
                    T[slot][x, PAD + L : PAD + L + 1, :] = jnp.zeros((1, LANES), f32)

            def load_warm(x, c):
                for b in range(LB):
                    place = pl.ds(b * SUB * R + x, SUB, stride=R)
                    put_theta(0, 0, x, b, warm_flat[place, :])
                return c

            lax.fori_loop(0, R, load_warm, 0)
            start(th_moves(0), ts_sem.at[0], tr_sem.at[0])

    vel_back = [
        pltpu.make_async_copy(vel_st.at[f], vel_out.at[f], loc_sem.at[f]) for f in range(2)
    ]
    for cp in vel_back:
        cp.start()

    finish(vel_moves(SWEEPS), vs_sem.at[SWEEPS], vr_sem.at[SWEEPS])
    prepare(SWEEPS)

    def heat_row(x):
        ice = icy[pl.ds(x, 1), :].astype(f32)
        for b in range(LB):
            bl = b * SUB
            effective, visc = strain(SWEEPS % 2, x, b)[:2]
            Q[0, x, bl : bl + SUB, :] = (ice * 0.1) * visc * effective

    def heat_body(i, c):
        for j in range(STEP):
            heat_row(i * STEP + j)
        return c

    lax.fori_loop(0, R // STEP, heat_body, 0)

    outs = []
    for k in range(SECTIONS):
        finish(th_moves(k), ts_sem.at[k], tr_sem.at[k])
        for side, row in ((0, 0), (1, R + 1)):
            T[k % 2][row, PAD : PAD + L, :] = trow_rx[k, side]
        for b in range(LB):
            bl = b * SUB
            tmh[bl : bl + SUB, :] = jnp.where(
                odd, roll(tcol_rx[k, 0, bl : bl + SUB, :], 2), tcol_rx[k, 1, bl : bl + SUB, :]
            )
        if k < SECTIONS - 1:
            section(k, 0, R)
            continue
        for c in range(R // SUB):
            section(k, c * SUB, SUB)
            for d in list(range(1, m)) + [0]:
                to = lax.rem(g + d, m)
                src = warm_st.at[pl.ds(to * LG, LG), c * SUB : (c + 1) * SUB, :]
                dst = temp_out.at[
                    :,
                    c * SUB : (c + 1) * SUB,
                    pl.ds(pl.multiple_of(g * LANES, LANES), LANES),
                ]
                if d == 0:
                    cp = pltpu.make_async_copy(src, dst, os_sem.at[c, 0])
                else:
                    cp = pltpu.make_async_remote_copy(
                        src,
                        dst,
                        os_sem.at[c, d],
                        or_sem.at[c, d],
                        device_id=(t, to),
                        device_id_type=MESH,
                    )
                cp.start()
                outs.append(cp)
    hard_back = pltpu.make_async_copy(hard_st, hard_out, loc_sem.at[2])
    hard_back.start()
    for cp in outs:
        cp.wait()
    for cp in vel_back:
        cp.wait()
    hard_back.wait()


def local(n, m, vel, rate, warm, grav, slide, icy, bed):
    _, L, R, Y = vel.shape
    LG = L // m
    assert Y == LANES and 4 * R <= LANES and R % SUB == 0 and L % (SUB * m) == 0
    f32 = jnp.float32
    any_spec = pl.BlockSpec(memory_space=pl.ANY)
    vmem = pl.BlockSpec(memory_space=pltpu.VMEM)
    K = SWEEPS + 1
    V = pltpu.VMEM
    dma = pltpu.SemaphoreType.DMA
    return pl.pallas_call(
        functools.partial(kernel, n, m, R, L, LG),
        out_shape=(
            jax.ShapeDtypeStruct(vel.shape, f32),
            jax.ShapeDtypeStruct(warm.shape, f32),
            jax.ShapeDtypeStruct(rate.shape, f32),
        ),
        in_specs=[any_spec] * 3 + [vmem] * 4,
        out_specs=(any_spec,) * 3,
        scratch_shapes=[
            V((2, L, R, LANES), f32),
            V((L, R, LANES), f32),
            V((L, R, LANES), f32),
            V((L, R, LANES), f32),
            V((2, R + 2, L + 2 * PAD, LANES), f32),
            V((2, R + 2, L + 2 * PAD, LANES), f32),
            V((2, R + 2, L, LANES), f32),
            V((2, R, L, LANES), f32),
            V((R + 2, L + 2 * PAD, LANES), f32),
            V((R + 2, L + 2 * PAD, LANES), f32),
            V((L, LANES), f32),
            V((L, LANES), f32),
            V((2, R, L, LANES), f32),
            V((K, L, LANES), f32),
            V((SWEEPS, 2, SUB, LANES), f32),
            V((K, 2, 2, L, LANES), f32),
            V((K, 2, L, LANES), f32),
            V((SWEEPS, 2, 2, SUB, LANES), f32),
            V((SECTIONS, L, LANES), f32),
            V((SECTIONS, 2, L, LANES), f32),
            V((SECTIONS, 2, L, LANES), f32),
            dma((4,)),
            dma((K, 8)),
            dma((K, 8)),
            dma((SECTIONS, 4)),
            dma((SECTIONS, 4)),
            dma((m,)),
            dma((m,)),
            dma((R // SUB, m)),
            dma((R // SUB, m)),
        ],
        compiler_params=pltpu.CompilerParams(
            collective_id=0, has_side_effects=True, vmem_limit_bytes=60 * 1024 * 1024
        ),
        name="ice_step",
    )(vel, rate, warm, grav, slide, icy, bed)


def solution(mesh):
    return jax.shard_map(
        functools.partial(local, mesh.shape["tile"], mesh.shape["grp"]),
        mesh=mesh,
        in_specs=(
            P(None, None, "tile", "grp"),
            P(None, "tile", "grp"),
            P("grp", "tile", None),
            P(None, "tile", "grp"),
            P("tile", "grp"),
            P("tile", "grp"),
            P("tile", "grp"),
        ),
        out_specs=(P(None, None, "tile", "grp"), P("grp", "tile", None), P(None, "tile", "grp")),
        check_vma=False,
    )
```

```python
import functools

import jax
import jax.numpy as jnp
from jax import lax
from jax.experimental import pallas as pl
from jax.experimental.pallas import tpu as pltpu
from jax.sharding import PartitionSpec as P

SWEEPS = 4
SECTIONS = 4
LANES = 128
SUB = 8
PAD = 8

MESH = pl.DeviceIdType.MESH


def roll(x, shift, axis=1):
    return pltpu.roll(x, shift, axis)


def kernel(
    n,
    m,
    R,
    L,
    LG,
    vel_in,
    rate_in,
    warm_in,
    grav,
    slide,
    icy,
    bed,
    vel_out,
    temp_out,
    hard_out,
    vel_st,
    rate_st,
    warm_st,
    hard_st,
    U0,
    U1,
    DY,
    SY,
    T0,
    T1,
    mh,
    tmh,
    Q,
    pk,
    dk,
    row_rx,
    col_rx,
    diag_rx,
    tpk,
    trow_rx,
    tcol_rx,
    loc_sem,
    vs_sem,
    vr_sem,
    ts_sem,
    tr_sem,
    ws_sem,
    wr_sem,
    os_sem,
    or_sem,
):
    t = lax.axis_index("tile")
    g = lax.axis_index("grp")
    LB = L // SUB
    U = (U0, U1)
    T = (T0, T1)
    STEP = 2
    WIDE = 4
    f32 = jnp.float32

    vel_cp = [
        pltpu.make_async_copy(vel_in.at[f], vel_st.at[f], loc_sem.at[f]) for f in range(2)
    ]
    rate_cp = pltpu.make_async_copy(rate_in, rate_st, loc_sem.at[2])
    for cp in vel_cp:
        cp.start()
    rate_cp.start()

    lo_t, hi_t, lo_g, hi_g = t > 0, t < n - 1, g > 0, g < m - 1

    def has(dt, dg):
        ok = None
        for d, lo, hi in ((dt, lo_t, hi_t), (dg, lo_g, hi_g)):
            if d:
                c = lo if d < 0 else hi
                ok = c if ok is None else jnp.logical_and(ok, c)
        return ok

    for ref in (row_rx, col_rx, diag_rx, trow_rx, tcol_rx):
        ref[...] = jnp.zeros_like(ref)

    barrier = pltpu.get_barrier_semaphore()
    around = [(-1, -1), (-1, 0), (-1, 1), (1, -1), (1, 0), (1, 1)]
    for dt, dg in around:

        @pl.when(has(dt, dg))
        def _(dt=dt, dg=dg):
            pl.semaphore_signal(
                barrier, inc=1, device_id=(t + dt, g + dg), device_id_type=MESH
            )

    for d in range(1, m):
        pl.semaphore_signal(
            barrier, inc=1, device_id=(t, lax.rem(g + d, m)), device_id_type=MESH
        )

    sides_t = lo_t.astype(jnp.int32) + hi_t.astype(jnp.int32)
    sides_g = lo_g.astype(jnp.int32) + hi_g.astype(jnp.int32)
    pl.semaphore_wait(barrier, m - 1 + sides_t * (1 + sides_g))

    def warm_copy(d):
        to = lax.rem(g + d, m)
        src = warm_in.at[:, :, pl.ds(pl.multiple_of(to * LANES, LANES), LANES)]
        dst = warm_st.at[pl.ds(g * LG, LG)]
        if d == 0:
            return pltpu.make_async_copy(src, dst, loc_sem.at[3])
        return pltpu.make_async_remote_copy(
            src, dst, ws_sem.at[d], wr_sem.at[d], device_id=(t, to), device_id_type=MESH
        )

    lane = lax.broadcasted_iota(jnp.int32, (SUB, LANES), 1)
    subl = lax.broadcasted_iota(jnp.int32, (SUB, LANES), 0)
    first = lane == 0
    last = lane == LANES - 1
    odd = lax.rem(lane, 2) == 1
    half = LANES // 2
    u_edge = jnp.logical_or(first, last)

    def back(x, extra=0):
        return lax.rem(2 * LANES - 1 - 2 * x - extra, LANES)

    def near_lane(x, shift):
        lane_x = lax.rem(lane + (LANES + 1) - shift, LANES)
        return lane_x < 2

    def vel_moves(k):
        slot = k % 2
        moves = [
            ((1, 0), U[slot].at[:, R, PAD : PAD + L, :], row_rx.at[k, 0]),
            ((-1, 0), U[slot].at[:, 1, PAD : PAD + L, :], row_rx.at[k, 1]),
            ((0, 1), pk.at[k], col_rx.at[k, 0]),
            ((0, -1), pk.at[k], col_rx.at[k, 1]),
        ]
        if k < SWEEPS:
            moves += [
                ((1, 1), dk.at[k, 1], diag_rx.at[k, 0, 0]),
                ((1, -1), dk.at[k, 1], diag_rx.at[k, 0, 1]),
                ((-1, 1), dk.at[k, 0], diag_rx.at[k, 1, 0]),
                ((-1, -1), dk.at[k, 0], diag_rx.at[k, 1, 1]),
            ]
        return moves

    def start(moves, s_sem, r_sem, early=None):
        for j, ((dt, dg), src, dst) in enumerate(moves):
            if early is not None and early != (dt != 0):
                continue

            @pl.when(has(dt, dg))
            def _(j=j, dt=dt, dg=dg, src=src, dst=dst):
                pltpu.make_async_remote_copy(
                    src,
                    dst,
                    s_sem.at[j],
                    r_sem.at[j],
                    device_id=(t + dt, g + dg),
                    device_id_type=MESH,
                ).start()

    def finish(moves, s_sem, r_sem):
        for j, ((dt, dg), src, dst) in enumerate(moves):

            @pl.when(has(dt, dg))
            def _(j=j, dt=dt, dg=dg, src=src, dst=dst):
                pltpu.make_async_remote_copy(
                    src,
                    dst,
                    s_sem.at[j],
                    r_sem.at[j],
                    device_id=(t + dt, g + dg),
                    device_id_type=MESH,
                ).wait_send()

            @pl.when(has(-dt, -dg))
            def _(j=j, dt=dt, dg=dg, src=src, dst=dst):
                pltpu.make_async_remote_copy(
                    src,
                    dst,
                    s_sem.at[j],
                    r_sem.at[j],
                    device_id=(t - dt, g - dg),
                    device_id_type=MESH,
                ).wait_recv()

    def put_vel(slot, k, x, b, values):
        lv = PAD + b * SUB
        for f in range(2):
            U[slot][f, x + 1, lv : lv + SUB, :] = values[f]
            if b == 0:
                U[slot][f, x + 1, lv - 1 : lv, :] = values[f][0:1]
            if b == LB - 1:
                U[slot][f, x + 1, lv + SUB : lv + SUB + 1, :] = values[f][SUB - 1 : SUB]
        bl = b * SUB
        w = jnp.where(
            near_lane(x, 2 * x + half),
            roll(values[1], lax.rem(2 * x + half, LANES)),
            pk[k, bl : bl + SUB, :],
        )
        pk[k, bl : bl + SUB, :] = jnp.where(near_lane(x, 2 * x), roll(values[0], 2 * x), w)

    def put_diag(slot, k):
        for side, x in ((0, 1), (1, R)):
            acc = jnp.zeros((SUB, LANES), f32)
            for b in range(LB):
                lv = PAD + b * SUB
                u = U[slot][0, x, lv : lv + SUB, :]
                v = U[slot][1, x, lv : lv + SUB, :]
                w = jnp.where(u_edge, u, roll(v, half))
                w = roll(w, 2 * b) if b else w
                hit = jnp.logical_or(near_lane(b, 2 * b), near_lane(b, 2 * b + half))
                acc = jnp.where(hit, w, acc)
            dk[k, side] = acc

    def fill_level_pads(slot, row):
        for f in range(2):
            U[slot][f, row, PAD - 1 : PAD, :] = U[slot][f, row, PAD : PAD + 1, :]
            U[slot][f, row, PAD + L : PAD + L + 1, :] = U[slot][
                f, row, PAD + L - 1 : PAD + L, :
            ]

    def lane_parts(f, row, b, u, edge):
        up = jnp.where(last, edge, roll(u, LANES - 1))
        down = jnp.where(first, edge, roll(u, 1))
        bl = b * SUB
        DY[f, row, bl : bl + SUB, :] = up - down
        return up + down, bl

    def prepare(k):
        slot = k % 2
        for side, row in ((0, 0), (1, R + 1)):
            for f in range(2):
                U[slot][f, row, PAD : PAD + L, :] = row_rx[k, side, f]
            if k < SWEEPS:
                corner = jnp.where(odd, roll(diag_rx[k, side, 0], 2), diag_rx[k, side, 1])
                for b in range(LB):
                    lv = PAD + b * SUB
                    for f in range(2):
                        edge = roll(corner, (2 * LANES - 2 * b - 1 - f * half) % LANES)
                        lane_parts(f, row, b, U[slot][f, row, lv : lv + SUB, :], edge)

        for b in range(LB):
            bl = b * SUB
            mh[bl : bl + SUB, :] = jnp.where(
                odd, roll(col_rx[k, 0, bl : bl + SUB, :], 2), col_rx[k, 1, bl : bl + SUB, :]
            )

        def body(i, c):
            for b in range(LB):
                lv = PAD + b * SUB
                bl = b * SUB
                halo = mh[bl : bl + SUB, :]
                for x in [i * WIDE + j for j in range(WIDE)]:
                    for f in range(2):
                        edge = roll(halo, back(x, f * half))
                        u = U[slot][f, x + 1, lv : lv + SUB, :]
                        s, _ = lane_parts(f, x + 1, b, u, edge)
                        if k < SWEEPS:
                            SY[f, x, bl : bl + SUB, :] = s
            return c

        lax.fori_loop(0, R // WIDE, body, 0)

    def strain(slot, x, b):
        lv = PAD + b * SUB
        bl = b * SUB
        ue = U[slot][0, x + 2, lv : lv + SUB, :]
        uw = U[slot][0, x, lv : lv + SUB, :]
        ve = U[slot][1, x + 2, lv : lv + SUB, :]
        vw = U[slot][1, x, lv : lv + SUB, :]
        uu = U[slot][0, x + 1, lv + 1 : lv + 1 + SUB, :]
        ul = U[slot][0, x + 1, lv - 1 : lv - 1 + SUB, :]
        vu = U[slot][1, x + 1, lv + 1 : lv + 1 + SUB, :]
        vl = U[slot][1, x + 1, lv - 1 : lv - 1 + SUB, :]
        dyu = DY[0, x + 1, bl : bl + SUB, :]
        dyv = DY[1, x + 1, bl : bl + SUB, :]
        xx = ue - uw
        shear = dyu + (ve - vw)
        du = uu - ul
        dv = vu - vl
        effective = 0.25 * (
            xx * xx + dyv * dyv + xx * dyv + 0.25 * (shear * shear + du * du + dv * dv)
        )
        rate = Q[1, x, bl : bl + SUB, :]
        viscosity = rate * jnp.exp(jnp.log(effective + 0.01) * (-1.0 / 3.0))
        return effective, viscosity, ue + uw, ve + vw, uu + ul, vu + vl

    def sweep(k):
        slot = k % 2
        new_slot = (k + 1) % 2

        def row(x):
            ice = icy[pl.ds(x, 1), :].astype(f32)
            drag = slide[pl.ds(x, 1), :] * bed[pl.ds(x, 1), :].astype(f32)
            water = 1.0 - ice
            gu = grav[0, pl.ds(x, 1), :]
            gv = grav[1, pl.ds(x, 1), :]
            for b in range(LB):
                bl = b * SUB
                _, visc, sxu, sxv, szu, szv = strain(slot, x, b)
                diagonal = 22.0 * visc + water
                if b == 0:
                    diagonal = diagonal + jnp.where(subl == 0, drag, 0.0)
                cross_u = DY[1, x + 2, bl : bl + SUB, :] - DY[1, x, bl : bl + SUB, :]
                cross_v = DY[0, x + 2, bl : bl + SUB, :] - DY[0, x, bl : bl + SUB, :]
                near_u = 4.0 * (sxu + szu) + SY[0, x, bl : bl + SUB, :] + 0.75 * cross_u
                near_v = (
                    sxv + 4.0 * (SY[1, x, bl : bl + SUB, :] + szv) + 0.75 * cross_v
                )
                scale = ice / diagonal
                new_u = (gu + visc * near_u) * scale
                new_v = (gv + visc * near_v) * scale
                put_vel(new_slot, k + 1, x, b, (new_u, new_v))
                if k == SWEEPS - 1:
                    place = pl.ds(bl * R + x, SUB, stride=R)
                    vel_flat[0][place, :] = new_u
                    vel_flat[1][place, :] = new_v

        def body(i, c):
            row(i)
            row(R - 1 - i)
            return c

        lax.fori_loop(0, 1, body, 0)
        if k + 1 < SWEEPS:
            put_diag(new_slot, k + 1)
        moves = vel_moves(k + 1), vs_sem.at[k + 1], vr_sem.at[k + 1]
        start(*moves, early=True)
        lax.fori_loop(1, R // 2, body, 0)
        start(*moves, early=False)

    def th_moves(k):
        slot = k % 2
        return [
            ((1, 0), T[slot].at[R, PAD : PAD + L, :], trow_rx.at[k, 0]),
            ((-1, 0), T[slot].at[1, PAD : PAD + L, :], trow_rx.at[k, 1]),
            ((0, 1), tpk.at[k], tcol_rx.at[k, 0]),
            ((0, -1), tpk.at[k], tcol_rx.at[k, 1]),
        ]

    def put_theta(slot, k, x, b, value):
        lv = PAD + b * SUB
        bl = b * SUB
        T[slot][x + 1, lv : lv + SUB, :] = value
        w = roll(value, 2 * x)
        tpk[k, bl : bl + SUB, :] = jnp.where(
            near_lane(x, 2 * x), w, tpk[k, bl : bl + SUB, :]
        )

    def section(k, x0, rows):
        slot = k % 2
        new_slot = (k + 1) % 2

        def row(x):
            for b in range(LB):
                lv = PAD + b * SUB
                bl = b * SUB
                edge = roll(tmh[bl : bl + SUB, :], back(x))
                center = T[slot][x + 1, lv : lv + SUB, :]
                north = jnp.where(last, edge, roll(center, LANES - 1))
                south = jnp.where(first, edge, roll(center, 1))
                east = T[slot][x + 2, lv : lv + SUB, :]
                west = T[slot][x, lv : lv + SUB, :]
                upper = T[slot][x + 1, lv + 1 : lv + 1 + SUB, :]
                lower = T[slot][x + 1, lv - 1 : lv - 1 + SUB, :]
                u = U[SWEEPS % 2][0, x + 1, lv : lv + SUB, :]
                v = U[SWEEPS % 2][1, x + 1, lv : lv + SUB, :]
                advect = (
                    jnp.maximum(u, 0.0) * (center - west)
                    + jnp.minimum(u, 0.0) * (east - center)
                    + jnp.maximum(v, 0.0) * (center - south)
                    + jnp.minimum(v, 0.0) * (north - center)
                )
                value = (
                    center
                    + 0.1 * (east + west + north + south - 4.0 * center)
                    + 0.2 * (upper + lower - 2.0 * center)
                    - 0.05 * advect
                    + Q[0, x, bl : bl + SUB, :]
                )
                if k < SECTIONS - 1:
                    put_theta(new_slot, k + 1, x, b, value)
                else:
                    place = pl.ds(bl * R + x, SUB, stride=R)
                    warm_flat[place, :] = value
                    hard_flat[place, :] = jnp.exp(-0.6 * value)

        if k == SECTIONS - 1:

            def chunk(i, c):
                for j in range(STEP):
                    row(x0 + i * STEP + j)
                return c

            lax.fori_loop(0, rows // STEP, chunk, 0)
            return

        def body(i, c):
            row(i)
            row(R - 1 - i)
            return c

        lax.fori_loop(0, 1, body, 0)
        moves = th_moves(k + 1), ts_sem.at[k + 1], tr_sem.at[k + 1]
        start(*moves, early=True)
        lax.fori_loop(1, R // 2, body, 0)
        start(*moves, early=False)

    vel_flat = [vel_st.at[f].reshape(L * R, LANES) for f in range(2)]
    rate_flat = rate_st.reshape(L * R, LANES)
    warm_flat = warm_st.reshape(L * R, LANES)
    hard_flat = hard_st.reshape(L * R, LANES)

    for cp in vel_cp:
        cp.wait()

    def load_vel(x, c):
        for b in range(LB):
            place = pl.ds(b * SUB * R + x, SUB, stride=R)
            put_vel(0, 0, x, b, (vel_flat[0][place, :], vel_flat[1][place, :]))
        return c

    pk[...] = jnp.zeros_like(pk)
    tpk[...] = jnp.zeros_like(tpk)
    lax.fori_loop(0, R, load_vel, 0)
    put_diag(0, 0)
    start(vel_moves(0), vs_sem.at[0], vr_sem.at[0])
    warm = [warm_copy(d) for d in range(m)]
    warm[0].start()
    rate_cp.wait()

    def load_rate(x, c):
        for b in range(LB):
            place = pl.ds(b * SUB * R + x, SUB, stride=R)
            Q[1, x, b * SUB : (b + 1) * SUB, :] = rate_flat[place, :]
        return c

    lax.fori_loop(0, R, load_rate, 0)

    for k in range(SWEEPS):
        finish(vel_moves(k), vs_sem.at[k], vr_sem.at[k])
        for cp in warm[1 + k :] if k == SWEEPS - 1 else warm[1 + k : 2 + k]:
            cp.start()
        prepare(k)
        sweep(k)
        if k == SWEEPS - 1:
            for cp in warm:
                cp.wait()
            for slot in range(2):
                for x in range(R + 2):
                    T[slot][x, PAD - 1 : PAD, :] = jnp.zeros((1, LANES), f32)
                    T[slot][x, PAD + L : PAD + L + 1, :] = jnp.zeros((1, LANES), f32)

            def load_warm(x, c):
                for b in range(LB):
                    place = pl.ds(b * SUB * R + x, SUB, stride=R)
                    put_theta(0, 0, x, b, warm_flat[place, :])
                return c

            lax.fori_loop(0, R, load_warm, 0)
            start(th_moves(0), ts_sem.at[0], tr_sem.at[0])

    vel_back = [
        pltpu.make_async_copy(vel_st.at[f], vel_out.at[f], loc_sem.at[f]) for f in range(2)
    ]
    for cp in vel_back:
        cp.start()

    finish(vel_moves(SWEEPS), vs_sem.at[SWEEPS], vr_sem.at[SWEEPS])
    prepare(SWEEPS)

    def heat_row(x):
        ice = icy[pl.ds(x, 1), :].astype(f32)
        for b in range(LB):
            bl = b * SUB
            effective, visc = strain(SWEEPS % 2, x, b)[:2]
            Q[0, x, bl : bl + SUB, :] = (ice * 0.1) * visc * effective

    def heat_body(i, c):
        for j in range(STEP):
            heat_row(i * STEP + j)
        return c

    lax.fori_loop(0, R // STEP, heat_body, 0)

    outs = []
    for k in range(SECTIONS):
        finish(th_moves(k), ts_sem.at[k], tr_sem.at[k])
        for side, row in ((0, 0), (1, R + 1)):
            T[k % 2][row, PAD : PAD + L, :] = trow_rx[k, side]
        for b in range(LB):
            bl = b * SUB
            tmh[bl : bl + SUB, :] = jnp.where(
                odd, roll(tcol_rx[k, 0, bl : bl + SUB, :], 2), tcol_rx[k, 1, bl : bl + SUB, :]
            )
        if k < SECTIONS - 1:
            section(k, 0, R)
            continue
        for c in range(R // SUB):
            section(k, c * SUB, SUB)
            for d in sorted(range(1, m), key=lambda d: -min(d, m - d)) + [0]:
                to = lax.rem(g + d, m)
                src = warm_st.at[pl.ds(to * LG, LG), c * SUB : (c + 1) * SUB, :]
                dst = temp_out.at[
                    :,
                    c * SUB : (c + 1) * SUB,
                    pl.ds(pl.multiple_of(g * LANES, LANES), LANES),
                ]
                if d == 0:
                    cp = pltpu.make_async_copy(src, dst, os_sem.at[c, 0])
                else:
                    cp = pltpu.make_async_remote_copy(
                        src,
                        dst,
                        os_sem.at[c, d],
                        or_sem.at[c, d],
                        device_id=(t, to),
                        device_id_type=MESH,
                    )
                cp.start()
                outs.append(cp)
    hard_back = pltpu.make_async_copy(hard_st, hard_out, loc_sem.at[2])
    hard_back.start()
    for cp in outs:
        cp.wait()
    for cp in vel_back:
        cp.wait()
    hard_back.wait()


def local(n, m, vel, rate, warm, grav, slide, icy, bed):
    _, L, R, Y = vel.shape
    LG = L // m
    assert Y == LANES and 4 * R <= LANES and R % SUB == 0 and L % (SUB * m) == 0
    f32 = jnp.float32
    any_spec = pl.BlockSpec(memory_space=pl.ANY)
    vmem = pl.BlockSpec(memory_space=pltpu.VMEM)
    K = SWEEPS + 1
    V = pltpu.VMEM
    dma = pltpu.SemaphoreType.DMA
    return pl.pallas_call(
        functools.partial(kernel, n, m, R, L, LG),
        out_shape=(
            jax.ShapeDtypeStruct(vel.shape, f32),
            jax.ShapeDtypeStruct(warm.shape, f32),
            jax.ShapeDtypeStruct(rate.shape, f32),
        ),
        in_specs=[any_spec] * 3 + [vmem] * 4,
        out_specs=(any_spec,) * 3,
        scratch_shapes=[
            V((2, L, R, LANES), f32),
            V((L, R, LANES), f32),
            V((L, R, LANES), f32),
            V((L, R, LANES), f32),
            V((2, R + 2, L + 2 * PAD, LANES), f32),
            V((2, R + 2, L + 2 * PAD, LANES), f32),
            V((2, R + 2, L, LANES), f32),
            V((2, R, L, LANES), f32),
            V((R + 2, L + 2 * PAD, LANES), f32),
            V((R + 2, L + 2 * PAD, LANES), f32),
            V((L, LANES), f32),
            V((L, LANES), f32),
            V((2, R, L, LANES), f32),
            V((K, L, LANES), f32),
            V((SWEEPS, 2, SUB, LANES), f32),
            V((K, 2, 2, L, LANES), f32),
            V((K, 2, L, LANES), f32),
            V((SWEEPS, 2, 2, SUB, LANES), f32),
            V((SECTIONS, L, LANES), f32),
            V((SECTIONS, 2, L, LANES), f32),
            V((SECTIONS, 2, L, LANES), f32),
            dma((4,)),
            dma((K, 8)),
            dma((K, 8)),
            dma((SECTIONS, 4)),
            dma((SECTIONS, 4)),
            dma((m,)),
            dma((m,)),
            dma((R // SUB, m)),
            dma((R // SUB, m)),
        ],
        compiler_params=pltpu.CompilerParams(
            collective_id=0, has_side_effects=True, vmem_limit_bytes=60 * 1024 * 1024
        ),
        name="ice_step",
    )(vel, rate, warm, grav, slide, icy, bed)


def solution(mesh):
    return jax.shard_map(
        functools.partial(local, mesh.shape["tile"], mesh.shape["grp"]),
        mesh=mesh,
        in_specs=(
            P(None, None, "tile", "grp"),
            P(None, "tile", "grp"),
            P("grp", "tile", None),
            P(None, "tile", "grp"),
            P("tile", "grp"),
            P("tile", "grp"),
            P("tile", "grp"),
        ),
        out_specs=(P(None, None, "tile", "grp"), P("grp", "tile", None), P(None, "tile", "grp")),
        check_vma=False,
    )
```
